128 devices in a mesh: section: 4 (over x_hi, core), dom: 32 (over z, y, x_lo).
Axes of the slice: x: 4 (x_hi: 2, x_lo: 2; x = x_hi * 2 + x_lo), y: 4, z: 4, core: 2. Of those that a mesh axis runs over, the one named last changes fastest.
Arguments:
- initial_features: bfloat16 [49152, 384], P('dom'), may hold values from -16 to 16
- layer_weights: bfloat16 [8, 384, 384], P('section'), may hold values from -0.3125 to 0.3125
- adjacency_tiles: bfloat16 [384, 24, 128, 128], P('dom'), may hold values from -0.15625 to 0.15625
- tile_columns: int32 [384, 24], P('dom'), may hold values from 0 to 107, as said below
- send_blocks: int32 [32, 3, 32], P('dom'), may hold values from -1 to 3, as said below
- stale_imports: bfloat16 [8, 32, 64, 128, 384], P('section', 'dom'), may hold values from 0 to 1.5
Outputs:
- final_features: bfloat16 [49152, 384], P('dom', 'section')
The draws below stay inside these ranges and needn't reach their ends.
Inputs may be any that keep to these rules, and one draw needn't show every extreme that they name: send_blocks[q, h, p] is -1 when q equals p, else -1 or a block index of 0 to 3 within row group h. `tile_columns`: for a tile of partition p's local block r: a value j < 12 names p's own block j with j // 4 <= r // 4; a value 12 + h*32 + q names an import slot with send_blocks[q, h, p] >= 0.
All inputs are finite; a program needn't handle non-finite values.
Results may differ from the reference program's by a relative error of at most 0.011.
Values may be sent and summed in bfloat16 or wider, within the bound.
A program may use at most 256 MiB of HBM per device.

```python
import jax
import jax.numpy as jnp
from jax import lax

D = 384
BLOCK = 128
TILES = 24
GROUPS = 3
GROUP_BLOCKS = 4
PARTITIONS = 32
LAYERS = 8
BLOCKS_DEV = 12
NBLK = 384
SLOTS = 96
STALE_SLOTS = 64
NODES = 49152


def graph_tables(key):
    base = jax.random.fold_in(key, 311)
    key_use, key_pick, key_score = jax.random.split(base, 3)
    usable = jax.random.randint(key_use, (PARTITIONS, GROUPS, PARTITIONS), 0, 5) < 3
    usable = usable.at[PARTITIONS - 1, GROUPS - 1, 0].set(True)
    picks = jax.random.randint(key_pick, (PARTITIONS, GROUPS, PARTITIONS), 0, GROUP_BLOCKS)
    diagonal = jnp.arange(PARTITIONS)[:, None, None] == jnp.arange(PARTITIONS)[None, None, :]
    sends = jnp.where(usable & ~diagonal, picks, -1).astype(jnp.int32)
    row_group = jnp.arange(BLOCKS_DEV) // GROUP_BLOCKS
    own_ok = jnp.arange(BLOCKS_DEV)[None, :] // GROUP_BLOCKS <= row_group[:, None]
    import_ok = (sends >= 0).transpose(2, 1, 0).reshape(PARTITIONS, SLOTS)
    own_full = jnp.broadcast_to(own_ok[None, :, :], (PARTITIONS, BLOCKS_DEV, BLOCKS_DEV))
    import_full = jnp.broadcast_to(import_ok[:, None, :], (PARTITIONS, BLOCKS_DEV, SLOTS))
    valid = jnp.concatenate([own_full, import_full], -1)
    total = BLOCKS_DEV + SLOTS
    scores = jax.random.randint(key_score, (PARTITIONS, BLOCKS_DEV, TILES, total), 0, 1 << 20) * 256
    scores = scores + jnp.arange(total, dtype=jnp.int32)[None, None, None, :]
    scores = jnp.where(valid[:, :, None, :], scores, -1)
    columns = jnp.argmax(scores, -1).astype(jnp.int32).reshape(NBLK, TILES)
    columns = columns.at[BLOCKS_DEV - 1, 0].set(total - 1)
    columns = columns.at[0, 0].set(0)
    return (sends, columns.astype(jnp.int32))


def draw_tile_columns(key, part):
    return graph_tables(key)[1]


def draw_send_blocks(key, part):
    return graph_tables(key)[0]


def block_scale(stream_key, dims, cuts, low, top_value):
    factor_of = 1.0
    for dim, parts in cuts:
        steps = jax.random.uniform(jax.random.fold_in(jax.random.fold_in(stream_key, 6), dim), (parts,), jnp.float32, low / len(cuts), top_value / len(cuts))
        factor_of = factor_of * jnp.repeat(jnp.exp(steps), dims[dim] // parts).reshape((-1,) + (1,) * (len(dims) - 1 - dim))
    return factor_of


def gaussian(key, shape, spread, reach, cuts=(), kind=jnp.bfloat16):
    drawn = jax.random.normal(key, shape, jnp.float32) * spread
    if len(cuts) > 0:
        drawn = block_scale(key, shape, cuts, -0.22, 0.18) * drawn
    return jnp.clip(drawn, min=-reach, max=reach).astype(kind)


def setup_inputs(seed: int = 0) -> dict:
    keys = jax.random.split(jax.random.key(seed), 7)
    initial_features = gaussian(keys[0], (NODES, D), 4.0, 16.0, ((0, 32),))
    layer_weights = gaussian(keys[1], (LAYERS, D, D), D ** -0.5, 0.3125, ((0, 4),))
    adjacency_tiles = gaussian(keys[2], (NBLK, TILES, BLOCK, BLOCK), (TILES * BLOCK // 2) ** -0.5, 0.15625, ((0, 32),))
    tile_columns = draw_tile_columns(jax.random.fold_in(keys[6], 71), 0)
    send_blocks = draw_send_blocks(jax.random.fold_in(keys[6], 71), 0)
    stale_imports = jnp.clip(1.5 * jax.random.uniform(keys[5], (LAYERS, PARTITIONS, STALE_SLOTS, BLOCK, D), jnp.float32) ** block_scale(keys[5], (LAYERS, PARTITIONS, STALE_SLOTS, BLOCK, D), ((0, 4), (1, 32)), -0.2, 0.2), 0.0, 1.5).astype(jnp.bfloat16)
    return dict(initial_features=initial_features, layer_weights=layer_weights, adjacency_tiles=adjacency_tiles, tile_columns=tile_columns, send_blocks=send_blocks, stale_imports=stale_imports)


alpha_mix = 0.1
lambda_decay = 0.5


def finish(summed, initial_rows, weight, beta_layer):
    mixed = ((1.0 - alpha_mix) * summed + alpha_mix * initial_rows.astype(jnp.float32)).astype(jnp.bfloat16)
    flat = mixed.reshape(-1, mixed.shape[-1])
    product = jnp.dot(flat, weight, preferred_element_type=jnp.float32).reshape(mixed.shape)
    return jax.nn.relu((1.0 - beta_layer) * mixed.astype(jnp.float32) + beta_layer * product).astype(jnp.bfloat16)


def reference(initial_features, layer_weights, adjacency_tiles, tile_columns, send_blocks, stale_imports):
    part_total = PARTITIONS
    initial = initial_features.reshape(part_total, BLOCKS_DEV, BLOCK, D)
    tile_blocks = adjacency_tiles.reshape(part_total, BLOCKS_DEV, TILES, BLOCK, BLOCK)
    column_blocks = tile_columns.reshape(part_total, BLOCKS_DEV, TILES)
    offsets = jnp.arange(GROUPS, dtype=jnp.int32)[None, :, None] * GROUP_BLOCKS
    source_rows = (jnp.maximum(send_blocks, 0) + offsets).astype(jnp.int32)
    present = send_blocks >= 0
    slot_group = jnp.arange(SLOTS, dtype=jnp.int32) // PARTITIONS
    part_ids = jnp.arange(part_total, dtype=jnp.int32)[:, None, None]

    def one_layer(features, inputs):
        weight, stale_layer, layer_index = inputs
        beta_layer = jnp.log(lambda_decay / (layer_index.astype(jnp.float32) + 1.0) + 1.0)
        picked = features[part_ids, source_rows]
        picked = jnp.where(present[..., None, None], picked, jnp.zeros_like(picked))
        fresh_all = picked.transpose(2, 1, 0, 3, 4).reshape(part_total, SLOTS, BLOCK, D)

        def per_part(pieces):
            own_blocks, fresh_part, stale_part, init_part, tile_part, column_part = pieces
            stale_full = jnp.concatenate([jnp.zeros((PARTITIONS, BLOCK, D), jnp.bfloat16), stale_part], 0)
            finished = []
            for group_index in range(GROUPS):
                imports = jnp.where((slot_group <= group_index)[:, None, None], fresh_part, stale_full)
                table = jnp.concatenate([own_blocks, imports], 0)
                low = group_index * GROUP_BLOCKS
                high = low + GROUP_BLOCKS
                gathered = table[column_part[low:high]]
                summed = jnp.einsum("rkij,rkjd->rid", tile_part[low:high].astype(jnp.float32), gathered.astype(jnp.float32))
                finished.append(finish(summed, init_part[low:high], weight, beta_layer))
            return jnp.concatenate(finished, 0)

        advanced = lax.map(per_part, (features, fresh_all, stale_layer, initial, tile_blocks, column_blocks))
        return advanced, None

    result, unused = lax.scan(one_layer, initial, (layer_weights, stale_imports, jnp.arange(LAYERS, dtype=jnp.int32)))
    return result.reshape(NODES, D)
```

```python
import jax
import jax.numpy as jnp
import numpy as np
from jax import lax
from jax.experimental import pallas as pl
from jax.experimental.pallas import tpu as pltpu
from jax.sharding import PartitionSpec as P

alpha_mix = 0.1
lambda_decay = 0.5

VMEM_LIMIT = 56 * 1024 * 1024


def stale_kernel(count_ref, tile_ref, col_ref, adj_ref, stale_ref, out_ref, acc_ref):
    row = pl.program_id(0)
    count = count_ref[row]
    acc_ref[...] = jnp.zeros_like(acc_ref)

    def body(step, carry):
        first, second = 2 * step, 2 * step + 1
        t0, t1 = tile_ref[row, first], tile_ref[row, second]
        c0, c1 = col_ref[row, first], col_ref[row, second]
        keep = second < count
        right = jnp.where(keep, adj_ref[0, t1], jnp.zeros_like(adj_ref[0, t1]))
        left = jnp.concatenate([adj_ref[0, t0], right], 1)
        for layer in range(2):
            rows = jnp.concatenate([stale_ref[layer, c0], stale_ref[layer, c1]], 0)
            acc_ref[layer] += jnp.dot(left, rows, preferred_element_type=jnp.float32)
        return carry

    lax.fori_loop(0, (count + 1) // 2, body, 0)
    out_ref[:, 0] = acc_ref[...]


def stale_sums(tile_columns, adjacency, stale, groups, group_blocks, part_count):
    blocks, fanout = tile_columns.shape
    block, width = stale.shape[2], stale.shape[3]
    own = blocks
    rows = (groups - 1) * group_blocks
    cols = tile_columns[:rows]
    row_group = (jnp.arange(rows, dtype=jnp.int32) // group_blocks)[:, None]
    is_stale = cols >= own + part_count * (row_group + 1)
    rank = jnp.cumsum(is_stale.astype(jnp.int32), 1)
    places = jnp.arange(fanout, dtype=jnp.int32)[None, None, :]
    hit = is_stale[:, :, None] & (rank[:, :, None] - 1 == places)
    tile_list = jnp.sum(jnp.where(hit, jnp.arange(fanout, dtype=jnp.int32)[None, :, None], 0), 1)
    col_list = jnp.sum(jnp.where(hit, (cols - own - part_count)[:, :, None], 0), 1)
    counts = rank[:, -1]
    return pl.pallas_call(
        stale_kernel,
        out_shape=jax.ShapeDtypeStruct((2, rows, block, width), jnp.float32),
        grid_spec=pltpu.PrefetchScalarGridSpec(
            num_scalar_prefetch=3,
            grid=(rows,),
            in_specs=[
                pl.BlockSpec((1, fanout, block, block), lambda r, *_: (r, 0, 0, 0)),
                pl.BlockSpec(memory_space=pltpu.VMEM),
            ],
            out_specs=pl.BlockSpec((2, 1, block, width), lambda r, *_: (0, r, 0, 0)),
            scratch_shapes=[pltpu.VMEM((2, block, width), jnp.float32)],
        ),
        compiler_params=pltpu.CompilerParams(vmem_limit_bytes=VMEM_LIMIT),
        name="stale_sums",
    )(counts, tile_list, col_list, adjacency, stale)


def gather_sums(layer, idx, flag, own, recv, adj, stale):
    blocks, piece, width = own.shape
    slots = recv.shape[0]
    block = adj.shape[1]
    pieces = block // piece
    stale_rows = stale.shape[1]

    def kernel(idx_ref, flag_ref, own_ref, recv_ref, adj_ref, stale_ref, out_ref, table, rhs, sems):
        row = pl.program_id(0)
        fanout = idx_ref.shape[1]

        @pl.when(row == 0)
        def _():
            first = pltpu.make_async_copy(own_ref, table.at[pl.ds(0, blocks)], sems.at[0])
            second = pltpu.make_async_copy(recv_ref, table.at[pl.ds(blocks, slots)], sems.at[1])
            first.start()
            second.start()
            table[blocks + slots] = jnp.zeros((piece, width), table.dtype)
            first.wait()
            second.wait()

        for t in range(fanout):
            rhs[pl.ds(t * piece, piece), :] = table[idx_ref[row, t]]
        total = jnp.dot(adj_ref[0], rhs[...], preferred_element_type=jnp.float32)
        use = (flag_ref[0] == layer // 2) & (row < stale_rows)
        total = total + jnp.where(use, stale_ref[0, 0], 0.0)
        out_ref[:, 0] = total.reshape(pieces, piece, width).astype(out_ref.dtype)

    return pl.pallas_call(
        kernel,
        out_shape=jax.ShapeDtypeStruct((pieces, blocks, piece, width), jnp.bfloat16),
        grid_spec=pltpu.PrefetchScalarGridSpec(
            num_scalar_prefetch=2,
            grid=(blocks,),
            in_specs=[
                pl.BlockSpec(memory_space=pl.ANY),
                pl.BlockSpec(memory_space=pl.ANY),
                pl.BlockSpec((1, block, adj.shape[2]), lambda r, *_: (r, 0, 0)),
                pl.BlockSpec(
                    (1, 1, block, width),
                    lambda r, *_: (layer % 2, jnp.minimum(r, stale_rows - 1), 0, 0),
                ),
            ],
            out_specs=pl.BlockSpec((pieces, 1, piece, width), lambda r, *_: (0, r, 0, 0)),
            scratch_shapes=[
                pltpu.VMEM((blocks + slots + 1, piece, width), jnp.bfloat16),
                pltpu.VMEM((adj.shape[2], width), jnp.bfloat16),
                pltpu.SemaphoreType.DMA((2,)),
            ],
        ),
        compiler_params=pltpu.CompilerParams(vmem_limit_bytes=VMEM_LIMIT),
        name="gather_sums",
    )(idx, flag, own, recv, adj, stale)


def pack(picks_ref, features_ref, out_ref, groups, group_blocks):
    dests = out_ref.shape[0]

    def body(dest, carry):
        for h in range(groups):
            out_ref[dest, h] = features_ref[h * group_blocks + picks_ref[h, dest]]
        return carry

    lax.fori_loop(0, dests, body, 0)


def pack_first(picks, features, groups, group_blocks):
    blocks, piece, width = features.shape
    dests = picks.shape[1]

    def kernel(picks_ref, features_ref, out_ref):
        pack(picks_ref, features_ref, out_ref, groups, group_blocks)

    return pl.pallas_call(
        kernel,
        out_shape=jax.ShapeDtypeStruct((dests, groups, piece, width), jnp.bfloat16),
        in_specs=[pl.BlockSpec(memory_space=pltpu.SMEM), pl.BlockSpec(memory_space=pltpu.VMEM)],
        out_specs=pl.BlockSpec(memory_space=pltpu.VMEM),
        compiler_params=pltpu.CompilerParams(vmem_limit_bytes=VMEM_LIMIT),
        name="pack_first",
    )(picks, features)


def combine(layer, last, beta, picks, parts, initial, weight, groups, group_blocks):
    pieces, blocks, piece, width = parts.shape
    dests = picks.shape[1]

    def kernel(picks_ref, parts_ref, initial_ref, weight_ref, next_ref, *outs):
        for block in range(blocks):
            summed = parts_ref[0, block].astype(jnp.float32)
            for part in range(1, pieces):
                summed = summed + parts_ref[part, block].astype(jnp.float32)
            mixed = ((1.0 - alpha_mix) * summed + alpha_mix * initial_ref[block].astype(jnp.float32))
            mixed = mixed.astype(jnp.bfloat16)
            product = jnp.dot(mixed, weight_ref[...], preferred_element_type=jnp.float32)
            value = (1.0 - beta) * mixed.astype(jnp.float32) + beta * product
            next_ref[block] = jnp.maximum(value, 0.0).astype(jnp.bfloat16)
        if outs:
            pack(picks_ref, next_ref, outs[0], groups, group_blocks)

    shapes = [jax.ShapeDtypeStruct((blocks, piece, width), jnp.bfloat16)]
    if not last:
        shapes.append(jax.ShapeDtypeStruct((dests, groups, piece, width), jnp.bfloat16))
    return pl.pallas_call(
        kernel,
        out_shape=shapes,
        in_specs=[pl.BlockSpec(memory_space=pltpu.SMEM)] + [pl.BlockSpec(memory_space=pltpu.VMEM)] * 3,
        out_specs=[pl.BlockSpec(memory_space=pltpu.VMEM)] * len(shapes),
        compiler_params=pltpu.CompilerParams(vmem_limit_bytes=VMEM_LIMIT),
        name="combine",
    )(picks, parts, initial, weight)


def per_device(
    initial_features, layer_weights, adjacency_tiles, tile_columns, send_blocks, stale_imports
):
    section = lax.axis_index("section")
    sections = lax.axis_size("section")
    part_count = lax.axis_size("dom")
    blocks, fanout, block = adjacency_tiles.shape[:3]
    width = initial_features.shape[1]
    groups = send_blocks.shape[1]
    group_blocks = blocks // groups
    depth = layer_weights.shape[0]
    layers = depth * sections
    piece = block // sections
    slots = groups * part_count

    weights = lax.all_gather(layer_weights, "section", axis=0, tiled=True)
    adj = lax.dynamic_slice_in_dim(adjacency_tiles, section * piece, piece, 3)
    adj = adj.transpose(0, 2, 1, 3).reshape(blocks, block, fanout * piece)
    initial = lax.dynamic_slice_in_dim(
        initial_features.reshape(blocks, block, width), section * piece, piece, 1
    )
    picks = jnp.maximum(send_blocks[0], 0)
    row_group = (jnp.arange(blocks, dtype=jnp.int32) // group_blocks)[:, None]
    slot = jnp.maximum(tile_columns - blocks, 0)
    slot_group, slot_part = slot // part_count, slot % part_count
    idx = jnp.where(
        tile_columns < blocks,
        tile_columns,
        jnp.where(slot_group <= row_group, blocks + slot_part * groups + slot_group, blocks + slots),
    )
    stale = stale_sums(
        tile_columns, adjacency_tiles, stale_imports[:, 0], groups, group_blocks, part_count
    )
    flag = section[None].astype(jnp.int32)

    features = initial
    outgoing = pack_first(picks, initial, groups, group_blocks)
    for layer in range(layers):
        received = lax.all_to_all(outgoing, "dom", split_axis=0, concat_axis=0, tiled=True)
        received = received.reshape(slots, piece, width)
        parts = gather_sums(layer, idx, flag, features, received, adj, stale)
        parts = lax.all_to_all(parts, "section", split_axis=0, concat_axis=0, tiled=True)
        beta = float(np.log(np.float32(lambda_decay) / np.float32(layer + 1) + np.float32(1.0)))
        last = layer == layers - 1
        outs = combine(layer, last, beta, picks, parts, initial, weights[layer], groups, group_blocks)
        features = outs[0]
        if not last:
            outgoing = outs[1]

    columns = width // sections
    split = features.reshape(blocks, piece, sections, columns).transpose(2, 0, 1, 3)
    joined = lax.all_to_all(split, "section", split_axis=0, concat_axis=0, tiled=True)
    return joined.transpose(1, 0, 2, 3).reshape(blocks * block, columns)


def solution(mesh):
    return jax.shard_map(
        per_device,
        mesh=mesh,
        in_specs=(
            P("dom", None),
            P("section", None, None),
            P("dom", None, None, None),
            P("dom", None),
            P("dom", None, None),
            P("section", "dom", None, None, None),
        ),
        out_specs=P("dom", "section"),
        check_vma=False,
    )
```

```python
import jax
import jax.numpy as jnp
import numpy as np
from jax import lax
from jax.experimental import pallas as pl
from jax.experimental.pallas import tpu as pltpu
from jax.sharding import PartitionSpec as P

alpha_mix = 0.1
lambda_decay = 0.5

VMEM_LIMIT = 56 * 1024 * 1024


def stale_kernel(count_ref, tile_ref, col_ref, adj_ref, stale_ref, out_ref, acc_ref):
    row = pl.program_id(0)
    count = count_ref[row]
    acc_ref[...] = jnp.zeros_like(acc_ref)

    def body(step, carry):
        first, second = 2 * step, 2 * step + 1
        t0, t1 = tile_ref[row, first], tile_ref[row, second]
        c0, c1 = col_ref[row, first], col_ref[row, second]
        keep = second < count
        right = jnp.where(keep, adj_ref[0, t1], jnp.zeros_like(adj_ref[0, t1]))
        left = jnp.concatenate([adj_ref[0, t0], right], 1)
        for layer in range(2):
            rows = jnp.concatenate([stale_ref[layer, c0], stale_ref[layer, c1]], 0)
            acc_ref[layer] += jnp.dot(left, rows, preferred_element_type=jnp.float32)
        return carry

    lax.fori_loop(0, (count + 1) // 2, body, 0)
    out_ref[:, 0] = acc_ref[...]


def stale_sums(tile_columns, adjacency, stale, groups, group_blocks, part_count):
    blocks, fanout = tile_columns.shape
    block, width = stale.shape[2], stale.shape[3]
    own = blocks
    rows = (groups - 1) * group_blocks
    cols = tile_columns[:rows]
    row_group = (jnp.arange(rows, dtype=jnp.int32) // group_blocks)[:, None]
    is_stale = cols >= own + part_count * (row_group + 1)
    rank = jnp.cumsum(is_stale.astype(jnp.int32), 1)
    places = jnp.arange(fanout, dtype=jnp.int32)[None, None, :]
    hit = is_stale[:, :, None] & (rank[:, :, None] - 1 == places)
    tile_list = jnp.sum(jnp.where(hit, jnp.arange(fanout, dtype=jnp.int32)[None, :, None], 0), 1)
    col_list = jnp.sum(jnp.where(hit, (cols - own - part_count)[:, :, None], 0), 1)
    counts = rank[:, -1]
    return pl.pallas_call(
        stale_kernel,
        out_shape=jax.ShapeDtypeStruct((2, rows, block, width), jnp.float32),
        grid_spec=pltpu.PrefetchScalarGridSpec(
            num_scalar_prefetch=3,
            grid=(rows,),
            in_specs=[
                pl.BlockSpec((1, fanout, block, block), lambda r, *_: (r, 0, 0, 0)),
                pl.BlockSpec(memory_space=pltpu.VMEM),
            ],
            out_specs=pl.BlockSpec((2, 1, block, width), lambda r, *_: (0, r, 0, 0)),
            scratch_shapes=[pltpu.VMEM((2, block, width), jnp.float32)],
        ),
        compiler_params=pltpu.CompilerParams(vmem_limit_bytes=VMEM_LIMIT),
        name="stale_sums",
    )(counts, tile_list, col_list, adjacency, stale)


MESH = pl.DeviceIdType.MESH
GROUPS = 3
STAGES = 7


def slice_kernel(adj_ref, own_sel_ref, other_sel_ref, own_ref, other_ref):
    per = own_sel_ref.shape[0] // adj_ref.shape[2]
    for m in range(adj_ref.shape[1] // per):
        left = jnp.concatenate([adj_ref[0, m * per + u] for u in range(per)], 1)
        lanes = pl.ds(m * 128, 128)
        own_ref[0, :, lanes] = jnp.dot(
            left, own_sel_ref[...], preferred_element_type=jnp.float32
        ).astype(jnp.bfloat16)
        other_ref[0, :, lanes] = jnp.dot(
            left, other_sel_ref[...], preferred_element_type=jnp.float32
        ).astype(jnp.bfloat16)


def slice_tiles(adjacency, own_slice, other_slice, piece):
    blocks, fanout, block, _ = adjacency.shape
    per = block // piece
    source = jnp.arange(per * block, dtype=jnp.int32)[:, None]
    lane = jnp.arange(block, dtype=jnp.int32)[None, :]

    def selector(j):
        wanted = (lane // piece) * block + j * piece + lane % piece
        return (source == wanted).astype(jnp.bfloat16)

    shape = jax.ShapeDtypeStruct((blocks, block, fanout * piece), jnp.bfloat16)
    spec = pl.BlockSpec((1, block, fanout * piece), lambda r: (r, 0, 0))
    whole = pl.BlockSpec((per * block, block), lambda r: (0, 0))
    return pl.pallas_call(
        slice_kernel,
        out_shape=[shape, shape],
        grid=(blocks,),
        in_specs=[pl.BlockSpec((1, fanout, block, block), lambda r: (r, 0, 0, 0)), whole, whole],
        out_specs=[spec, spec],
        compiler_params=pltpu.CompilerParams(vmem_limit_bytes=VMEM_LIMIT),
        name="slice_tiles",
    )(adjacency, selector(own_slice), selector(other_slice))


def place():
    section, dom = lax.axis_index("section"), lax.axis_index("dom")
    x_hi, core = section // 2, section % 2
    z, y, x_lo = dom // 8, (dom // 2) % 4, dom % 2
    return section, dom, x_hi, core, z, y, x_lo


def piece_of(x_hi, x_lo, core):
    first = (1 - core) * ((x_lo + x_hi) % 2) + core * x_hi
    second = (1 - core) * x_hi + core * x_lo
    return first, second


def main_kernel(
    idx_ref, pick_ref, beta_ref, adj_ref, weight_ref, initial_ref, stale_ref, out_ref,
    table, part, *rest,
):
    rest = list(rest)

    def take(count):
        got = rest[:count]
        del rest[:count]
        return got

    xown, seltab, agbuf, out2, rel2, land2 = (take(GROUPS) for _ in range(6))
    send0, recv0, send1, recv1, send2, recv2, keep1, keep2 = (take(GROUPS) for _ in range(8))
    ag1_s, ag1_r, ag2_s, ag2_r, rel_s, rel_r, main_s, main_r, fwd_s, fwd_r, rs_s, rs_r = rest

    layers = weight_ref.shape[0]
    fanout = idx_ref.shape[0] // (2 * 4 * GROUPS)
    width = weight_ref.shape[1]
    section, dom, x_hi, core, z, y, x_lo = place()
    first, second = piece_of(x_hi, x_lo, core)
    a = (1 - core) * z + core * y
    b = (1 - core) * y + core * z
    zero_core, one_core = 1 - core, core

    def at(zz, yy, lo):
        return zz * 8 + yy * 2 + lo

    def on_a(step):
        return (section, at((z + zero_core * step) % 4, (y + one_core * step) % 4, x_lo))

    def on_b(step):
        return (section, at((z + one_core * step) % 4, (y + zero_core * step) % 4, x_lo))

    a_next = (on_a(1), on_a(3))
    b_next = (on_b(1), on_b(3))
    partner = (x_hi * 2 + 1 - core, dom)
    flip1 = (section, at(z, y, 1 - x_lo))
    flip3 = ((1 - x_hi) * 2 + core, at(z, y, 1 - x_lo))
    hi1 = zero_core * x_hi + one_core * (1 - x_hi)
    line1 = (hi1 * 2 + core, at(z, y, 1 - x_lo))
    hi2 = zero_core * (1 - x_hi) + one_core * x_hi
    line2 = (hi2 * 2 + core, at(z, y, 1 - x_lo))

    barrier = pltpu.get_barrier_semaphore()
    friends = (*a_next, *b_next, partner, flip1, flip3)
    for friend in friends:
        pl.semaphore_signal(barrier, inc=1, device_id=friend, device_id_type=MESH)
    pl.semaphore_wait(barrier, len(friends))

    def remote(src, dst, ssem, rsem, device):
        return pltpu.make_async_remote_copy(
            src_ref=src, dst_ref=dst, send_sem=ssem, recv_sem=rsem,
            device_id=device, device_id_type=MESH,
        )

    def ag1(g, par, d):
        return remote(xown[g], agbuf[g].at[par, d], ag1_s.at[g * 2 + d],
                      ag1_r.at[g * 4 + par * 2 + d], a_next[d])

    def ag2(g, par, d):
        return remote(agbuf[g].at[par, d, d], agbuf[g].at[par, 2, d], ag2_s.at[g * 2 + d],
                      ag2_r.at[g * 4 + par * 2 + d], a_next[d])

    def relay(g, par, d):
        return remote(out2[g].at[2, d], rel2[g].at[par, d], rel_s.at[g * 2 + d],
                      rel_r.at[g * 4 + par * 2 + d], b_next[d])

    def main(g, par, d):
        return remote(out2[g].at[d], land2[g].at[par, d], main_s.at[g * 2 + d],
                      main_r.at[g * 4 + par * 2 + d], b_next[d])

    def fwd(g, par, d):
        return remote(rel2[g].at[par, d], land2[g].at[par, 2, d], fwd_s.at[g * 2 + d],
                      fwd_r.at[g * 4 + par * 2 + d], b_next[d])

    def rs(stage, g, par):
        send, recv = ((send0, recv0), (send1, recv1), (send2, recv2))[stage]
        device = (partner, line1, line2)[stage]
        return remote(send[g], recv[g].at[par], rs_s.at[stage * GROUPS + g],
                      rs_r.at[(stage * GROUPS + g) * 2 + par], device)

    def stage_a(g, layer):
        par = layer % 2
        for d in range(2):
            ag1(g, par, d).wait_recv()
        for d in range(2):
            ag2(g, par, d).start()

    def stage_b(g, layer):
        par = layer % 2
        for d in range(2):
            seltab[g][(a + (3, 1)[d]) % 4] = agbuf[g][par, d]
        for d in range(2):
            ag1(g, par, d).wait_send()
            ag2(g, par, d).wait_recv()
        seltab[g][(a + 2) % 4] = agbuf[g][par, 2]

        def chosen(dest, half, line, lo):
            place_in = (((g * 4 + dest) * 2 + half) * 4 + line) * 2 + lo
            return seltab[g][line, lo, pick_ref[place_in]]

        for d in (2, 0, 1):
            dest = (b + (1, 3, 2)[d]) % 4
            for half in range(2):
                for line in range(4):
                    for lo in range(2):
                        out2[g][d, half, line, lo] = chosen(dest, half, line, lo)
            if d == 2:
                for e in range(2):
                    relay(g, par, e).start()
            else:
                main(g, par, d).start()
        for half in range(2):
            for line in range(4):
                for lo in range(2):
                    slot = 4 * GROUPS + g * 32 + b * 8 + line * 2 + lo
                    table[half, slot] = chosen(b, half, line, lo)

    def stage_c(g, layer):
        par = layer % 2
        for d in range(2):
            relay(g, par, d).wait_recv()
            fwd(g, par, d).start()
        for d in range(2):
            ag2(g, par, d).wait_send()

    def stage_d(g, layer):
        par = layer % 2

        def fill(rel, where):
            for half in range(2):
                slots = pl.ds(4 * GROUPS + g * 32 + where * 8, 8)
                table[half, slots] = land2[g][par, rel, half].reshape(8, 16, width)

        for half in range(2):
            table[half, pl.ds(4 * g, 4)] = xown[g][half]
        for d in range(2):
            main(g, par, d).wait_recv()
            fill(d, (b + (3, 1)[d]) % 4)
        for d in range(2):
            fwd(g, par, d).wait_recv()
        fill(2, (b + 2) % 4)

        for half in range(2):
            def row_block(j, carry, half=half):
                row = g * 4 + j
                base = (half * 4 * GROUPS + row) * fanout
                rows = jnp.concatenate([table[half, idx_ref[base + t]] for t in range(fanout)], 0)
                total = jnp.dot(adj_ref[half, row], rows, preferred_element_type=jnp.float32)
                part[half * 4 + j] = total.reshape(8, 16, width)
                return carry

            lax.fori_loop(0, 4, row_block, 0, unroll=True)

        if g < GROUPS - 1:
            @pl.when(section == layer // 2)
            def _():
                for j in range(4):
                    part[x_lo * 4 + j] += stale_ref[layer % 2, g * 4 + j]

        for j in range(8):
            send0[g][j] = part[j, pl.ds((1 - core) * 4, 4)].astype(jnp.bfloat16)
        rs(0, g, par).start()
        for d in range(2):
            relay(g, par, d).wait_send()
            main(g, par, d).wait_send()

    def stage_e(g, layer):
        par = layer % 2
        rs(0, g, par).wait_recv()
        for j in range(8):
            gone = part[j, pl.ds(core * 4 + (1 - first) * 2, 2)]
            gone = gone + recv0[g][par, j, pl.ds((1 - first) * 2, 2)].astype(jnp.float32)
            send1[g][j] = gone.astype(jnp.bfloat16)
        rs(1, g, par).start()
        for j in range(8):
            kept = part[j, pl.ds(core * 4 + first * 2, 2)]
            keep1[g][j] = kept + recv0[g][par, j, pl.ds(first * 2, 2)].astype(jnp.float32)
        rs(0, g, par).wait_send()
        for d in range(2):
            fwd(g, par, d).wait_send()

    def stage_f(g, layer):
        par = layer % 2
        rs(1, g, par).wait_recv()
        for j in range(8):
            gone = keep1[g][j, 1 - second] + recv1[g][par, j, 1 - second].astype(jnp.float32)
            send2[g][j] = gone.astype(jnp.bfloat16)
        rs(2, g, par).start()
        for j in range(8):
            keep2[g][j] = keep1[g][j, second] + recv1[g][par, j, second].astype(jnp.float32)
        rs(1, g, par).wait_send()

    def stage_h(g, layer):
        par = layer % 2
        rs(2, g, par).wait_recv()
        summed = keep2[g][...] + recv2[g][par].astype(jnp.float32)
        start = jnp.concatenate([initial_ref[half, pl.ds(4 * g, 4)] for half in range(2)], 0)
        mixed = (1.0 - alpha_mix) * summed + alpha_mix * start.astype(jnp.float32)
        mixed = mixed.astype(jnp.bfloat16).reshape(8 * 16, width)
        beta = beta_ref[layer]
        product = jnp.dot(mixed, weight_ref[layer], preferred_element_type=jnp.float32)
        value = (1.0 - beta) * mixed.astype(jnp.float32) + beta * product
        value = jnp.maximum(value, 0.0).astype(jnp.bfloat16).reshape(2, 4, 16, width)
        rs(2, g, par).wait_send()

        @pl.when(layer < layers - 1)
        def _():
            xown[g][...] = value
            for d in range(2):
                ag1(g, 1 - par, d).start()
            seltab[g][a] = value

        @pl.when(layer == layers - 1)
        def _():
            for half in range(2):
                out_ref[half, pl.ds(4 * g, 4)] = value[half]

    for half in range(2):
        table[half, 4 * GROUPS + 96] = jnp.zeros((16, width), jnp.bfloat16)
    for g in range(GROUPS):
        for half in range(2):
            xown[g][half] = initial_ref[half, pl.ds(4 * g, 4)]
        for d in range(2):
            ag1(g, 0, d).start()
        for half in range(2):
            seltab[g][a, half] = initial_ref[half, pl.ds(4 * g, 4)]

    stages = (stage_a, stage_b, stage_c, stage_d, stage_e, stage_f, stage_h)
    offsets = (0, 2, 4)

    def body(layer, carry):
        for tick in range(STAGES):
            now = [(g, tick - offsets[g]) for g in range(GROUPS)]
            late = [(g, s + STAGES) for g, s in now if s < 0]
            due = [(g, s) for g, s in now if s >= 0]
            if late:
                @pl.when(layer > 0)
                def _(late=late):
                    for g, s in late:
                        stages[s](g, layer - 1)
            if due:
                @pl.when(layer < layers)
                def _(due=due):
                    for g, s in due:
                        stages[s](g, layer)
        return carry

    lax.fori_loop(0, layers + 1, body, 0)


def run_layers(idx, picks, betas, adj, weights, initial, stale):
    width = weights.shape[1]
    piece = initial.shape[2]
    dt = jnp.bfloat16
    slab = (piece, width)

    def each(shape, dtype=dt):
        return [pltpu.VMEM((*shape, *slab), dtype) for _ in range(GROUPS)]

    sems = pltpu.SemaphoreType.DMA
    scratch = [
        pltpu.VMEM((2, 4 * GROUPS + 97, *slab), dt),
        pltpu.VMEM((8, 8, *slab), jnp.float32),
        *each((2, 4)), *each((4, 2, 4)), *each((2, 3, 2, 4)),
        *each((3, 2, 4, 2)), *each((2, 2, 4, 2)), *each((2, 3, 2, 4, 2)),
        *each((8, 4)), *each((2, 8, 4)),
        *each((8, 2)), *each((2, 8, 2)),
        *each((8,)), *each((2, 8)),
        *each((8, 2), jnp.float32), *each((8,), jnp.float32),
        *[sems((count,)) for _ in range(5) for count in (2 * GROUPS, 4 * GROUPS)],
        sems((3 * GROUPS,)), sems((6 * GROUPS,)),
    ]
    smem = pl.BlockSpec(memory_space=pltpu.SMEM)
    vmem = pl.BlockSpec(memory_space=pltpu.VMEM)
    return pl.pallas_call(
        main_kernel,
        out_shape=jax.ShapeDtypeStruct(initial.shape, dt),
        in_specs=[smem] * 3 + [vmem] * 4,
        out_specs=vmem,
        scratch_shapes=scratch,
        compiler_params=pltpu.CompilerParams(
            vmem_limit_bytes=VMEM_LIMIT, collective_id=0, has_side_effects=True
        ),
        name="run_layers",
    )(idx, picks, betas, adj, weights, initial, stale)


def per_device(
    initial_features, layer_weights, adjacency_tiles, tile_columns, send_blocks, stale_imports
):
    section, dom, x_hi, core, z, y, x_lo = place()
    sections = lax.axis_size("section")
    part_count = lax.axis_size("dom")
    blocks, fanout, block = adjacency_tiles.shape[:3]
    width = initial_features.shape[1]
    groups = send_blocks.shape[1]
    group_blocks = blocks // groups
    depth = layer_weights.shape[0]
    layers = depth * sections
    piece = block // 8

    def number(hi, lo):
        first, second = piece_of(hi, lo, core)
        return core * 4 + first * 2 + second

    mine, theirs = number(x_hi, x_lo), number(x_hi, 1 - x_lo)
    swap = [(p, p + 1 - 2 * (p % 2)) for p in range(part_count)]

    def by_half(own, other):
        pair = jnp.stack([own, other])
        return jnp.where(x_lo == 0, pair, pair[::-1])

    weights = lax.all_gather(layer_weights, "section", axis=0, tiled=True)
    own_adj, other_adj = slice_tiles(adjacency_tiles, mine, theirs, piece)
    adj = by_half(own_adj, lax.ppermute(other_adj, "dom", swap))

    init_blocks = initial_features.reshape(blocks, 8, piece, width)
    own_init = lax.dynamic_index_in_dim(init_blocks, mine, 1, keepdims=False)
    other_init = lax.dynamic_index_in_dim(init_blocks, theirs, 1, keepdims=False)
    initial = by_half(own_init, lax.ppermute(other_init, "dom", swap))

    sends = lax.all_gather(send_blocks[0], "dom", axis=0, tiled=False)
    sends = jnp.maximum(sends, 0).reshape(4, 4, 2, groups, 4, 4, 2)
    zy = lax.dynamic_index_in_dim(sends, y, 1, keepdims=False)
    zy = lax.dynamic_index_in_dim(zy, z, 3, keepdims=False)
    yz = lax.dynamic_index_in_dim(sends, z, 0, keepdims=False)
    yz = lax.dynamic_index_in_dim(yz, y, 4, keepdims=False)
    picks = jnp.where(core == 0, zy, yz)
    picks = picks.transpose(2, 3, 4, 0, 1).reshape(-1).astype(jnp.int32)

    columns = by_half(tile_columns, lax.ppermute(tile_columns, "dom", swap))
    row_group = (jnp.arange(blocks, dtype=jnp.int32) // group_blocks)[None, :, None]
    slot = jnp.maximum(columns - blocks, 0)
    slot_group, source = slot // part_count, slot % part_count
    zs, ys, los = source // 8, (source // 2) % 4, source % 2
    where = jnp.where(core == 0, ys * 8 + zs * 2, zs * 8 + ys * 2) + los
    idx = jnp.where(
        columns < blocks,
        columns,
        jnp.where(
            slot_group <= row_group,
            blocks + slot_group * part_count + where,
            blocks + groups * part_count,
        ),
    ).reshape(-1).astype(jnp.int32)

    stale = stale_sums(
        tile_columns, adjacency_tiles, stale_imports[:, 0], groups, group_blocks, part_count
    )
    stale = stale.reshape(2, (groups - 1) * group_blocks, 8, piece, width)
    betas = jnp.log(lambda_decay / (jnp.arange(layers, dtype=jnp.float32) + 1.0) + 1.0)

    done = run_layers(idx, picks, betas, adj, weights, initial, stale)

    keep = jnp.where(x_lo == 0, done[0], done[1])
    give = jnp.where(x_lo == 0, done[1], done[0])
    pair = by_half(keep, lax.ppermute(give, "dom", swap))
    cols = width // sections
    split = pair.reshape(2, blocks, piece, sections, cols).transpose(3, 0, 1, 2, 4)
    joined = lax.all_to_all(split, "section", split_axis=0, concat_axis=0, tiled=True)
    order = [0] * 8
    for hi in range(2):
        for c in range(2):
            for lo in range(2):
                first, second = piece_of(hi, lo, c)
                order[c * 4 + first * 2 + second] = (hi * 2 + c) * 2 + lo
    joined = joined.reshape(8, blocks, piece, cols)
    joined = jnp.stack([joined[k] for k in order], 1)
    return joined.reshape(blocks * block, cols)


def solution(mesh):
    return jax.shard_map(
        per_device,
        mesh=mesh,
        in_specs=(
            P("dom", None),
            P("section", None, None),
            P("dom", None, None, None),
            P("dom", None),
            P("dom", None, None),
            P("section", "dom", None, None, None),
        ),
        out_specs=P("dom", "section"),
        check_vma=False,
    )
```

```python
import jax
import jax.numpy as jnp
import numpy as np
from jax import lax
from jax.experimental import pallas as pl
from jax.experimental.pallas import tpu as pltpu
from jax.sharding import PartitionSpec as P

alpha_mix = 0.1
lambda_decay = 0.5

VMEM_LIMIT = 56 * 1024 * 1024


def stale_kernel(count_ref, tile_ref, col_ref, adj_ref, stale_ref, out_ref, acc_ref):
    row = pl.program_id(0)
    count = count_ref[row]
    acc_ref[...] = jnp.zeros_like(acc_ref)

    def body(step, carry):
        first, second = 2 * step, 2 * step + 1
        t0, t1 = tile_ref[row, first], tile_ref[row, second]
        c0, c1 = col_ref[row, first], col_ref[row, second]
        keep = second < count
        right = jnp.where(keep, adj_ref[0, t1], jnp.zeros_like(adj_ref[0, t1]))
        left = jnp.concatenate([adj_ref[0, t0], right], 1)
        for layer in range(2):
            rows = jnp.concatenate([stale_ref[layer, c0], stale_ref[layer, c1]], 0)
            acc_ref[layer] += jnp.dot(left, rows, preferred_element_type=jnp.float32)
        return carry

    lax.fori_loop(0, (count + 1) // 2, body, 0)
    out_ref[:, 0] = acc_ref[...]


def stale_sums(tile_columns, adjacency, stale, groups, group_blocks, part_count):
    blocks, fanout = tile_columns.shape
    block, width = stale.shape[2], stale.shape[3]
    own = blocks
    rows = (groups - 1) * group_blocks
    cols = tile_columns[:rows]
    row_group = (jnp.arange(rows, dtype=jnp.int32) // group_blocks)[:, None]
    is_stale = cols >= own + part_count * (row_group + 1)
    rank = jnp.cumsum(is_stale.astype(jnp.int32), 1)
    places = jnp.arange(fanout, dtype=jnp.int32)[None, None, :]
    hit = is_stale[:, :, None] & (rank[:, :, None] - 1 == places)
    tile_list = jnp.sum(jnp.where(hit, jnp.arange(fanout, dtype=jnp.int32)[None, :, None], 0), 1)
    col_list = jnp.sum(jnp.where(hit, (cols - own - part_count)[:, :, None], 0), 1)
    counts = rank[:, -1]
    return pl.pallas_call(
        stale_kernel,
        out_shape=jax.ShapeDtypeStruct((2, rows, block, width), jnp.float32),
        grid_spec=pltpu.PrefetchScalarGridSpec(
            num_scalar_prefetch=3,
            grid=(rows,),
            in_specs=[
                pl.BlockSpec((1, fanout, block, block), lambda r, *_: (r, 0, 0, 0)),
                pl.BlockSpec(memory_space=pltpu.VMEM),
            ],
            out_specs=pl.BlockSpec((2, 1, block, width), lambda r, *_: (0, r, 0, 0)),
            scratch_shapes=[pltpu.VMEM((2, block, width), jnp.float32)],
        ),
        compiler_params=pltpu.CompilerParams(vmem_limit_bytes=VMEM_LIMIT),
        name="stale_sums",
    )(counts, tile_list, col_list, adjacency, stale)


MESH = pl.DeviceIdType.MESH
GROUPS = 3


def slice_kernel(adj_ref, own_sel_ref, give_sel_ref, own_ref, give_ref):
    per = own_sel_ref.shape[0] // adj_ref.shape[2]
    for m in range(adj_ref.shape[1] // per):
        left = jnp.concatenate([adj_ref[0, m * per + u] for u in range(per)], 1)
        lanes = pl.ds(m * 128, 128)
        own_ref[0, :, lanes] = jnp.dot(
            left, own_sel_ref[...], preferred_element_type=jnp.float32
        ).astype(jnp.bfloat16)
        give_ref[0, :, lanes] = jnp.dot(
            left, give_sel_ref[0], preferred_element_type=jnp.float32
        ).astype(jnp.bfloat16)


def slice_tiles(adjacency, own_slice, near_slice, far_slice, piece):
    blocks, fanout, block, _ = adjacency.shape
    per = block // piece
    source = jnp.arange(per * block, dtype=jnp.int32)[:, None]
    lane = jnp.arange(block, dtype=jnp.int32)[None, :]

    def selector(j):
        wanted = (lane // piece) * block + j * piece + lane % piece
        return (source == wanted).astype(jnp.bfloat16)

    shape = jax.ShapeDtypeStruct((blocks, block, fanout * piece), jnp.bfloat16)
    spec = pl.BlockSpec((1, block, fanout * piece), lambda r: (r, 0, 0))
    whole = pl.BlockSpec((per * block, block), lambda r: (0, 0))
    given = pl.BlockSpec((1, per * block, block), lambda r: ((r % 4) // 3, 0, 0))
    return pl.pallas_call(
        slice_kernel,
        out_shape=[shape, shape],
        grid=(blocks,),
        in_specs=[pl.BlockSpec((1, fanout, block, block), lambda r: (r, 0, 0, 0)), whole, given],
        out_specs=[spec, spec],
        compiler_params=pltpu.CompilerParams(vmem_limit_bytes=VMEM_LIMIT),
        name="slice_tiles",
    )(adjacency, selector(own_slice), jnp.stack([selector(near_slice), selector(far_slice)]))


def place():
    section, dom = lax.axis_index("section"), lax.axis_index("dom")
    x_hi, core = section // 2, section % 2
    z, y, x_lo = dom // 8, (dom // 2) % 4, dom % 2
    return section, dom, x_hi, core, z, y, x_lo


def main_kernel(
    idx_ref, pick_ref, beta_ref, adj_ref, give_ref, weight_ref, initial_ref, stale_ref,
    spread_ref, out_ref, table, part, weights, other, *rest,
):
    rest = list(rest)

    def take(count):
        got = rest[:count]
        del rest[:count]
        return got

    xown, seltab, agbuf, out2, land2 = (take(GROUPS) for _ in range(5))
    send0, recv0, sendx, recvx, keep, fin, finland = (take(GROUPS) for _ in range(7))
    (ag_s, ag_r, sel_s, sel_r, core_s, core_r, x_s, x_r, fin_s, fin_r,
     tile_s, tile_r, w_s, w_r, w_local) = rest

    layers = beta_ref.shape[0]
    fanout = idx_ref.shape[0] // (2 * 4 * GROUPS)
    width = weight_ref.shape[1]
    section, dom, x_hi, core, z, y, x_lo = place()
    x = x_hi * 2 + x_lo
    a = (1 - core) * z + core * y
    b = (1 - core) * y + core * z

    def on_a(step):
        zz, yy = (z + (1 - core) * step) % 4, (y + core * step) % 4
        return (section, zz * 8 + yy * 2 + x_lo)

    def on_b(step):
        zz, yy = (z + core * step) % 4, (y + (1 - core) * step) % 4
        return (section, zz * 8 + yy * 2 + x_lo)

    def on_x(step, other_core=0):
        xx = (x + step) % 4
        cc = (core + other_core) % 2
        return ((xx // 2) * 2 + cc, z * 8 + y * 2 + xx % 2)

    steps = (1, 3, 2)
    partner = on_x(0, 1)
    near = (section, z * 8 + y * 2 + 1 - x_lo)
    far = ((1 - x_hi) * 2 + core, z * 8 + y * 2 + 1 - x_lo)

    barrier = pltpu.get_barrier_semaphore()
    friends = [on_a(s) for s in steps] + [on_b(s) for s in steps] + [partner]
    friends += [on_x(s, c) for s in steps for c in range(2)]
    for friend in friends:
        pl.semaphore_signal(barrier, inc=1, device_id=friend, device_id_type=MESH)
    pl.semaphore_wait(barrier, len(friends))

    def remote(src, dst, ssem, rsem, device):
        return pltpu.make_async_remote_copy(
            src_ref=src, dst_ref=dst, send_sem=ssem, recv_sem=rsem,
            device_id=device, device_id_type=MESH,
        )

    def gather(g, par, d):
        return remote(xown[g], agbuf[g].at[par, d], ag_s.at[g * 3 + d],
                      ag_r.at[(g * 2 + par) * 3 + d], on_a(steps[d]))

    def choose(g, par, d):
        return remote(out2[g].at[d], land2[g].at[par, d], sel_s.at[g * 3 + d],
                      sel_r.at[(g * 2 + par) * 3 + d], on_b(steps[d]))

    def to_core(g, par):
        return remote(send0[g], recv0[g].at[par], core_s.at[g], core_r.at[g * 2 + par], partner)

    def to_x(g, par, d):
        return remote(sendx[g].at[d], recvx[g].at[par, d], x_s.at[g * 3 + d],
                      x_r.at[(g * 2 + par) * 3 + d], on_x(steps[d]))

    hops = [(s, c) for s in (1, 3, 2, 0) for c in range(2) if (s, c) != (0, 0)]

    def to_out(g, n):
        s, c = hops[n]
        target = (x + s) % 4
        return remote(fin[g].at[(target // 2) * 2 + (core + c) % 2, target % 2], finland[g].at[n],
                      fin_s.at[g * 7 + n], fin_r.at[g * 7 + n], on_x(s, c))

    def give_near(g):
        rows = pl.ds(4 * g, 3)
        return remote(give_ref.at[rows], other.at[rows], tile_s.at[g * 2], tile_r.at[g * 2], near)

    def give_far(g):
        rows = pl.ds(4 * g + 3, 1)
        return remote(give_ref.at[rows], other.at[rows], tile_s.at[g * 2 + 1],
                      tile_r.at[g * 2 + 1], far)

    far_section = (1 - x_hi) * 2 + core
    weight_keep = pltpu.make_async_copy(weight_ref, weights.at[section], w_local)
    weight_core = remote(weight_ref, weights.at[section], w_s.at[0], w_r.at[0], partner)
    weight_far = remote(weight_ref, weights.at[section], w_s.at[1], w_r.at[1], far)
    weight_pass = remote(weights.at[far_section], weights.at[far_section], w_s.at[2], w_r.at[2],
                         partner)

    def stage_a(g, layer):
        par = layer % 2
        for d in range(3):
            gather(g, par, d).wait_recv()
            seltab[g][(a + 4 - steps[d]) % 4] = agbuf[g][par, d]
        for d in (2, 0, 1):
            for half in range(2):
                for line in range(4):
                    for lo in range(2):
                        out2[g][d, half, line, lo] = chosen(
                            g, (b + steps[d]) % 4, half, line, lo
                        )
            choose(g, par, d).start()

    def chosen(g, dest, half, line, lo):
        which = (((g * 4 + dest) * 2 + half) * 4 + line) * 2 + lo
        return seltab[g][line, lo, pick_ref[which]]

    def stage_d(g, layer):
        par = layer % 2
        for half in range(2):
            table[half, pl.ds(4 * g, 4)] = xown[g][half]
            for line in range(4):
                for lo in range(2):
                    slot = 4 * GROUPS + g * 32 + b * 8 + line * 2 + lo
                    table[half, slot] = chosen(g, b, half, line, lo)
        for d in range(3):
            choose(g, par, d).wait_recv()
            slots = pl.ds(4 * GROUPS + g * 32 + ((b + 4 - steps[d]) % 4) * 8, 8)
            for half in range(2):
                table[half, slots] = land2[g][par, d, half].reshape(8, 16, width)

        @pl.when(layer == 0)
        def _():
            give_near(g).wait_recv()
            give_far(g).wait_recv()

        for tiles, half in ((adj_ref, x_lo), (other, 1 - x_lo)):
            def row_block(j, carry, tiles=tiles, half=half):
                row = g * 4 + j
                base = (half * 4 * GROUPS + row) * fanout
                rows = jnp.concatenate([table[half, idx_ref[base + t]] for t in range(fanout)], 0)
                total = jnp.dot(tiles[row], rows, preferred_element_type=jnp.float32)
                part[half * 4 + j] = total.reshape(8, 16, width)
                return carry

            lax.fori_loop(0, 4, row_block, 0, unroll=True)

        if g < GROUPS - 1:
            @pl.when(section == layer // 2)
            def _():
                for j in range(4):
                    part[x_lo * 4 + j] += stale_ref[layer % 2, g * 4 + j]

        for j in range(8):
            send0[g][j] = part[j, pl.ds((1 - core) * 4, 4)].astype(jnp.bfloat16)
        to_core(g, par).start()
        for d in range(3):
            gather(g, par, d).wait_send()

    def stage_e(g, layer):
        par = layer % 2
        to_core(g, par).wait_recv()

        def summed(j, piece):
            return part[j, core * 4 + piece] + recv0[g][par, j, piece].astype(jnp.float32)

        for d in (2, 0, 1):
            piece = (x + steps[d]) % 4
            for j in range(8):
                sendx[g][d, j] = summed(j, piece).astype(jnp.bfloat16)
            to_x(g, par, d).start()
        for j in range(8):
            keep[g][j] = summed(j, x)
        for d in range(3):
            choose(g, par, d).wait_send()

    def stage_h(g, layer):
        par = layer % 2
        total = keep[g][...]
        for d in range(3):
            to_x(g, par, d).wait_recv()
            total = total + recvx[g][par, d].astype(jnp.float32)
        start = jnp.concatenate([initial_ref[half, pl.ds(4 * g, 4)] for half in range(2)], 0)
        mixed = (1.0 - alpha_mix) * total + alpha_mix * start.astype(jnp.float32)
        mixed = mixed.astype(jnp.bfloat16).reshape(8 * 16, width)
        beta = beta_ref[layer]
        weight = weights[layer // 2, layer % 2]
        product = jnp.dot(mixed, weight, preferred_element_type=jnp.float32)
        value = (1.0 - beta) * mixed.astype(jnp.float32) + beta * product
        value = jnp.maximum(value, 0.0).astype(jnp.bfloat16)

        @pl.when(layer < layers - 1)
        def _():
            shaped = value.reshape(2, 4, 16, width)
            xown[g][...] = shaped
            for d in (2, 0, 1):
                gather(g, 1 - par, d).start()
            seltab[g][a] = shaped

        @pl.when(layer == layers - 1)
        def _():
            wide = jnp.dot(value, spread_ref[...], preferred_element_type=jnp.float32)
            wide = wide.astype(jnp.bfloat16)
            for target in range(4):
                lanes = wide[:, target * 128:(target + 1) * 128]
                fin[g][target] = lanes.reshape(2, 4, 16, 128)
            for n in range(len(hops)):
                to_out(g, n).start()

        to_core(g, par).wait_send()
        for d in range(3):
            to_x(g, par, d).wait_send()

    for half in range(2):
        table[half, 4 * GROUPS + 96] = jnp.zeros((16, width), jnp.bfloat16)
    for g in range(GROUPS):
        for half in range(2):
            xown[g][half] = initial_ref[half, pl.ds(4 * g, 4)]
        for d in (2, 0, 1):
            gather(g, 0, d).start()
        for half in range(2):
            seltab[g][a, half] = initial_ref[half, pl.ds(4 * g, 4)]
    weight_keep.start()
    weight_core.start()
    give_near(0).start()
    give_far(0).start()
    weight_far.start()
    for g in range(1, GROUPS):
        give_near(g).start()
        give_far(g).start()

    def body(layer, carry):
        for g in range(GROUPS):
            if g == 2:
                @pl.when(layer == 0)
                def _():
                    weight_pass.wait_recv()

            for stage, back in ORDER:
                turn = g - back
                if turn >= 0:
                    @pl.when(layer < layers)
                    def _(stage=stage, turn=turn):
                        run[stage](turn, layer)
                else:
                    @pl.when(layer > 0)
                    def _(stage=stage, turn=turn):
                        run[stage](turn + GROUPS, layer - 1)

            if g == 0:
                @pl.when(layer == 0)
                def _():
                    weight_far.wait_recv()
                    weight_pass.start()
                    weight_keep.wait()
                    weight_core.wait_recv()
        return carry

    run = {"a": stage_a, "d": stage_d, "e": stage_e, "h": stage_h}
    lax.fori_loop(0, layers + 1, body, 0)

    for g in range(GROUPS):
        rows = pl.ds(4 * g, 4)
        mine = fin[g][section, x_lo]
        out_ref[rows, core * 4 + x] = mine
        for n, (s, c) in enumerate(hops):
            to_out(g, n).wait_recv()
            piece = ((core + c) % 2) * 4 + (x + 4 - s) % 4
            out_ref[rows, piece] = finland[g][n]
        for n in range(len(hops)):
            to_out(g, n).wait_send()
        give_near(g).wait_send()
        give_far(g).wait_send()
    weight_core.wait_send()
    weight_far.wait_send()
    weight_pass.wait_send()


ORDER = (("a", 0), ("d", 1), ("h", 2), ("e", 1))


def run_layers(idx, picks, betas, adj, give, weights, initial, stale, spread):
    depth, width = weights.shape[:2]
    blocks, piece = initial.shape[1:3]
    dt = jnp.bfloat16
    slab = (piece, width)

    def each(shape, dtype=dt, tail=slab):
        return [pltpu.VMEM((*shape, *tail), dtype) for _ in range(GROUPS)]

    sems = pltpu.SemaphoreType.DMA
    scratch = [
        pltpu.VMEM((2, 4 * GROUPS + 97, *slab), dt),
        pltpu.VMEM((8, 8, *slab), jnp.float32),
        pltpu.VMEM((4, *weights.shape), dt),
        pltpu.VMEM(adj.shape, dt),
        *each((2, 4)), *each((4, 2, 4)), *each((2, 3, 2, 4)),
        *each((3, 2, 4, 2)), *each((2, 3, 2, 4, 2)),
        *each((8, 4)), *each((2, 8, 4)),
        *each((3, 8)), *each((2, 3, 8)), *each((8,), jnp.float32),
        *each((4, 2, 4), dt, (piece, 128)), *each((7, 4), dt, (piece, 128)),
        sems((9,)), sems((18,)), sems((9,)), sems((18,)), sems((3,)), sems((6,)),
        sems((9,)), sems((18,)), sems((21,)), sems((21,)), sems((6,)), sems((6,)),
        sems((3,)), sems((3,)), sems,
    ]
    smem = pl.BlockSpec(memory_space=pltpu.SMEM)
    vmem = pl.BlockSpec(memory_space=pltpu.VMEM)
    return pl.pallas_call(
        main_kernel,
        out_shape=jax.ShapeDtypeStruct((blocks, 8, piece, 128), dt),
        in_specs=[smem] * 3 + [vmem] * 6,
        out_specs=vmem,
        scratch_shapes=scratch,
        compiler_params=pltpu.CompilerParams(
            vmem_limit_bytes=VMEM_LIMIT, collective_id=0, has_side_effects=True
        ),
        name="run_layers",
    )(idx, picks, betas, adj, give, weights, initial, stale, spread)


def per_device(
    initial_features, layer_weights, adjacency_tiles, tile_columns, send_blocks, stale_imports
):
    section, dom, x_hi, core, z, y, x_lo = place()
    sections = lax.axis_size("section")
    part_count = lax.axis_size("dom")
    blocks, fanout, block = adjacency_tiles.shape[:3]
    width = initial_features.shape[1]
    groups = send_blocks.shape[1]
    group_blocks = blocks // groups
    layers = layer_weights.shape[0] * sections
    piece = block // 8

    def number(hi, lo):
        return core * 4 + hi * 2 + lo

    mine = number(x_hi, x_lo)
    near, far = number(x_hi, 1 - x_lo), number(1 - x_hi, 1 - x_lo)
    swap = [(p, p + 1 - 2 * (p % 2)) for p in range(part_count)]

    def by_half(own, other):
        pair = jnp.stack([own, other])
        return jnp.where(x_lo == 0, pair, pair[::-1])

    init_blocks = initial_features.reshape(blocks, 8, piece, width)
    own_init = lax.dynamic_index_in_dim(init_blocks, mine, 1, keepdims=False)
    other_init = lax.dynamic_index_in_dim(init_blocks, near, 1, keepdims=False)
    other_init = lax.ppermute(other_init, "dom", swap)

    numbers = jnp.concatenate([send_blocks.reshape(-1), tile_columns.reshape(-1)])
    numbers = by_half(numbers, lax.ppermute(numbers, "dom", swap))
    sends = jnp.maximum(numbers[:, : groups * part_count], 0)
    columns = numbers[:, groups * part_count :].reshape(2, blocks, fanout)

    def along(step):
        moves = []
        for s in range(sections):
            for p in range(part_count):
                pz, py, lo = p // 8, (p // 2) % 4, p % 2
                q = (
                    ((pz + step) % 4) * 8 + py * 2 + lo
                    if s % 2 == 0
                    else pz * 8 + ((py + step) % 4) * 2 + lo
                )
                moves.append((s * part_count + p, s * part_count + q))
        return moves

    lines = jnp.stack(
        [sends] + [lax.ppermute(sends, ("section", "dom"), along(step)) for step in (1, 2, 3)]
    )
    a = jnp.where(core == 0, z, y)
    lines = lines[(a - jnp.arange(4, dtype=jnp.int32)) % 4]
    lines = lines.reshape(4, 2, groups, 4, 4, 2)
    to_y = lax.dynamic_index_in_dim(lines, z, 3, keepdims=False)
    to_z = lax.dynamic_index_in_dim(lines, y, 4, keepdims=False)
    picks = jnp.where(core == 0, to_y, to_z)
    picks = picks.transpose(2, 3, 4, 0, 1).reshape(-1).astype(jnp.int32)

    row_group = (jnp.arange(blocks, dtype=jnp.int32) // group_blocks)[None, :, None]
    slot = jnp.maximum(columns - blocks, 0)
    slot_group, source = slot // part_count, slot % part_count
    zs, ys, los = source // 8, (source // 2) % 4, source % 2
    where = jnp.where(core == 0, ys * 8 + zs * 2, zs * 8 + ys * 2) + los
    idx = jnp.where(
        columns < blocks,
        columns,
        jnp.where(
            slot_group <= row_group,
            blocks + slot_group * part_count + where,
            blocks + groups * part_count,
        ),
    ).reshape(-1).astype(jnp.int32)

    own_adj, give_adj = slice_tiles(adjacency_tiles, mine, near, far, piece)
    stale = stale_sums(
        tile_columns, adjacency_tiles, stale_imports[:, 0], groups, group_blocks, part_count
    )
    stale = stale.reshape(2, (groups - 1) * group_blocks, 8, piece, width)
    betas = jnp.log(lambda_decay / (jnp.arange(layers, dtype=jnp.float32) + 1.0) + 1.0)
    initial = by_half(own_init, other_init)
    cols = width // sections
    source = jnp.arange(width, dtype=jnp.int32)[:, None]
    lane = jnp.arange(sections * 128, dtype=jnp.int32)[None, :]
    spread = (source == (lane // 128) * cols + lane % 128) & (lane % 128 < cols)

    done = run_layers(
        idx, picks, betas, own_adj, give_adj, layer_weights, initial, stale,
        spread.astype(jnp.bfloat16),
    )
    return done.reshape(blocks * block, 128)[:, :cols]


def solution(mesh):
    return jax.shard_map(
        per_device,
        mesh=mesh,
        in_specs=(
            P("dom", None),
            P("section", None, None),
            P("dom", None, None, None),
            P("dom", None),
            P("dom", None, None),
            P("section", "dom", None, None, None),
        ),
        out_specs=P("dom", "section"),
        check_vma=False,
    )
```

```python
import jax
import jax.numpy as jnp
import numpy as np
from jax import lax
from jax.experimental import pallas as pl
from jax.experimental.pallas import tpu as pltpu
from jax.sharding import PartitionSpec as P

alpha_mix = 0.1
lambda_decay = 0.5

VMEM_LIMIT = 56 * 1024 * 1024


MESH = pl.DeviceIdType.MESH
GROUPS = 3


def place():
    section, dom = lax.axis_index("section"), lax.axis_index("dom")
    x_hi, core = section // 2, section % 2
    z, y, x_lo = dom // 8, (dom // 2) % 4, dom % 2
    return section, dom, x_hi, core, z, y, x_lo


def main_kernel(
    idx_ref, pick_ref, old_ref, beta_ref, tiles_ref, stale_ref, weight_ref, initial_ref,
    cut_ref, spread_ref, out_ref, table, part, weights, mine, give, other, tiles, stale, old, *rest,
):
    rest = list(rest)

    def take(count):
        got = rest[:count]
        del rest[:count]
        return got

    xown, seltab, agbuf, out2, land2 = (take(GROUPS) for _ in range(5))
    send0, recv0, sendx, recvx, keep, fin, finland = (take(GROUPS) for _ in range(7))
    (ag_s, ag_r, sel_s, sel_r, core_s, core_r, x_s, x_r, fin_s, fin_r,
     tile_s, tile_r, w_s, w_r, w_local, load) = rest

    layers = beta_ref.shape[0]
    fanout = idx_ref.shape[0] // (2 * 4 * GROUPS)
    width = weight_ref.shape[1]
    section, dom, x_hi, core, z, y, x_lo = place()
    x = x_hi * 2 + x_lo
    a = (1 - core) * z + core * y
    b = (1 - core) * y + core * z

    def on_a(step):
        zz, yy = (z + (1 - core) * step) % 4, (y + core * step) % 4
        return (section, zz * 8 + yy * 2 + x_lo)

    def on_b(step):
        zz, yy = (z + core * step) % 4, (y + (1 - core) * step) % 4
        return (section, zz * 8 + yy * 2 + x_lo)

    def on_x(step, other_core=0):
        xx = (x + step) % 4
        cc = (core + other_core) % 2
        return ((xx // 2) * 2 + cc, z * 8 + y * 2 + xx % 2)

    steps = (1, 3, 2)
    partner = on_x(0, 1)
    near = (section, z * 8 + y * 2 + 1 - x_lo)
    far = ((1 - x_hi) * 2 + core, z * 8 + y * 2 + 1 - x_lo)

    barrier = pltpu.get_barrier_semaphore()
    friends = [on_a(s) for s in steps] + [on_b(s) for s in steps] + [partner]
    friends += [on_x(s, c) for s in steps for c in range(2)]
    for friend in friends:
        pl.semaphore_signal(barrier, inc=1, device_id=friend, device_id_type=MESH)
    pl.semaphore_wait(barrier, len(friends))

    def remote(src, dst, ssem, rsem, device):
        return pltpu.make_async_remote_copy(
            src_ref=src, dst_ref=dst, send_sem=ssem, recv_sem=rsem,
            device_id=device, device_id_type=MESH,
        )

    def gather(g, par, d):
        return remote(xown[g], agbuf[g].at[par, d], ag_s.at[g * 3 + d],
                      ag_r.at[(g * 2 + par) * 3 + d], on_a(steps[d]))

    def choose(g, par, d, n):
        return remote(out2[g].at[d, n], land2[g].at[par, d, n], sel_s.at[(g * 3 + d) * 4 + n],
                      sel_r.at[((g * 2 + par) * 3 + d) * 4 + n], on_b(steps[d]))

    def to_core(g, par):
        return remote(send0[g], recv0[g].at[par], core_s.at[g], core_r.at[g * 2 + par], partner)

    def to_x(g, par, d):
        return remote(sendx[g].at[d], recvx[g].at[par, d], x_s.at[g * 3 + d],
                      x_r.at[(g * 2 + par) * 3 + d], on_x(steps[d]))

    hops = [(s, c) for s in (1, 3, 2, 0) for c in range(2) if (s, c) != (0, 0)]

    def to_out(g, n):
        s, c = hops[n]
        target = (x + s) % 4
        return remote(fin[g].at[(target // 2) * 2 + (core + c) % 2, target % 2], finland[g].at[n],
                      fin_s.at[g * 7 + n], fin_r.at[g * 7 + n], on_x(s, c))

    def give_near(g):
        rows = pl.ds(4 * g, 3)
        return remote(give.at[rows], other.at[rows], tile_s.at[g * 2], tile_r.at[g * 2], near)

    def give_far(g):
        rows = pl.ds(4 * g + 3, 1)
        return remote(give.at[rows], other.at[rows], tile_s.at[g * 2 + 1],
                      tile_r.at[g * 2 + 1], far)

    far_section = (1 - x_hi) * 2 + core
    weight_keep = pltpu.make_async_copy(weight_ref, weights.at[section], w_local)
    weight_core = remote(weight_ref, weights.at[section], w_s.at[0], w_r.at[0], partner)
    weight_far = remote(weight_ref, weights.at[section], w_s.at[1], w_r.at[1], far)
    weight_pass = remote(weights.at[far_section], weights.at[far_section], w_s.at[2], w_r.at[2],
                         partner)

    lines = [a] + [(a + 4 - step) % 4 for step in steps]

    def chosen(g, dest, half, n, lo):
        which = (((g * 4 + dest) * 2 + half) * 4 + lines[n]) * 2 + lo
        return seltab[g][n, lo, pick_ref[which]]

    def send_chosen(g, par, n):
        for d in (2, 0, 1):
            for half in range(2):
                for lo in range(2):
                    out2[g][d, n, half, lo] = chosen(g, (b + steps[d]) % 4, half, n, lo)
            choose(g, par, d, n).start()

    def stage_a(g, layer):
        par = layer % 2
        for d in range(3):
            gather(g, par, d).wait_recv()
            seltab[g][d + 1] = agbuf[g][par, d]
            send_chosen(g, par, d + 1)

    def slot_of(g, place_b, n):
        return 4 * GROUPS + g * 32 + place_b * 8 + lines[n] * 2

    def stage_d(g, layer):
        par = layer % 2
        for half in range(2):
            table[half, pl.ds(4 * g, 4)] = xown[g][half]
            for n in range(4):
                for lo in range(2):
                    table[half, slot_of(g, b, n) + lo] = chosen(g, b, half, n, lo)
        for n in range(4):
            for d in range(3):
                choose(g, par, d, n).wait_recv()
                slots = pl.ds(slot_of(g, (b + 4 - steps[d]) % 4, n), 2)
                for half in range(2):
                    table[half, slots] = land2[g][par, d, n, half]

        @pl.when(layer == 0)
        def _():
            give_near(g).wait_recv()
            give_far(g).wait_recv()

        for cut, half in ((mine, x_lo), (other, 1 - x_lo)):
            def row_block(j, carry, cut=cut, half=half):
                row = g * 4 + j
                base = (half * 4 * GROUPS + row) * fanout
                rows = jnp.concatenate([table[half, idx_ref[base + t]] for t in range(fanout)], 0)
                total = jnp.dot(cut[row], rows, preferred_element_type=jnp.float32)
                part[half * 4 + j] = total.reshape(8, 16, width)
                return carry

            lax.fori_loop(0, 4, row_block, 0, unroll=True)

        if g < GROUPS - 1:
            @pl.when(section == layer // 2)
            def _():
                for j in range(4):
                    part[x_lo * 4 + j] += old[j]

        for j in range(8):
            send0[g][j] = part[j, pl.ds((1 - core) * 4, 4)].astype(jnp.bfloat16)
        to_core(g, par).start()
        for d in range(3):
            gather(g, par, d).wait_send()

    def stage_e(g, layer):
        par = layer % 2
        to_core(g, par).wait_recv()

        def summed(j, piece):
            return part[j, core * 4 + piece] + recv0[g][par, j, piece].astype(jnp.float32)

        for d in (2, 0, 1):
            piece = (x + steps[d]) % 4
            for j in range(8):
                sendx[g][d, j] = summed(j, piece).astype(jnp.bfloat16)
            to_x(g, par, d).start()
        for j in range(8):
            keep[g][j] = summed(j, x)
        for d in range(3):
            for n in range(4):
                choose(g, par, d, n).wait_send()

    def stage_h(g, layer):
        par = layer % 2
        total = keep[g][...]
        for d in range(3):
            to_x(g, par, d).wait_recv()
            total = total + recvx[g][par, d].astype(jnp.float32)
        start = jnp.concatenate([initial_ref[half, pl.ds(4 * g, 4)] for half in range(2)], 0)
        mixed = (1.0 - alpha_mix) * total + alpha_mix * start.astype(jnp.float32)
        mixed = mixed.astype(jnp.bfloat16).reshape(8 * 16, width)
        beta = beta_ref[layer]
        weight = weights[layer // 2, layer % 2]
        product = jnp.dot(mixed, weight, preferred_element_type=jnp.float32)
        value = (1.0 - beta) * mixed.astype(jnp.float32) + beta * product
        value = jnp.maximum(value, 0.0).astype(jnp.bfloat16)

        @pl.when(layer < layers - 1)
        def _():
            shaped = value.reshape(2, 4, 16, width)
            xown[g][...] = shaped
            for d in (2, 0, 1):
                gather(g, 1 - par, d).start()
            seltab[g][0] = shaped
            send_chosen(g, 1 - par, 0)

        @pl.when(layer == layers - 1)
        def _():
            wide = jnp.dot(value, spread_ref[...], preferred_element_type=jnp.float32)
            wide = wide.astype(jnp.bfloat16)
            for target in range(4):
                lanes = wide[:, target * 128:(target + 1) * 128]
                fin[g][target] = lanes.reshape(2, 4, 16, 128)
            for n in range(len(hops)):
                to_out(g, n).start()

        to_core(g, par).wait_send()
        for d in range(3):
            to_x(g, par, d).wait_send()

    loads = []
    for g in range(GROUPS):
        rows = pl.ds(4 * g, 4)
        loads.append(pltpu.make_async_copy(tiles_ref.at[rows], tiles.at[rows], load.at[g]))
    for l in range(2):
        loads.append(
            pltpu.make_async_copy(stale_ref.at[l], stale.at[l, pl.ds(0, 64)], load.at[GROUPS + l])
        )
    for item in loads:
        item.start()
    for g in range(GROUPS):
        for half in range(2):
            xown[g][half] = initial_ref[half, pl.ds(4 * g, 4)]
        for d in (2, 0, 1):
            gather(g, 0, d).start()
        for half in range(2):
            seltab[g][0, half] = initial_ref[half, pl.ds(4 * g, 4)]
        send_chosen(g, 0, 0)
    weight_keep.start()
    weight_core.start()
    for half in range(2):
        table[half, 4 * GROUPS + 96] = jnp.zeros((16, width), jnp.bfloat16)
    for l in range(2):
        stale[l, 64] = jnp.zeros((128, width), jnp.bfloat16)

    def slice_rows(row, far_one):
        left = jnp.concatenate(
            [
                jnp.concatenate([tiles[row, m * 8 + u] for u in range(8)], 1)
                for m in range(fanout // 8)
            ],
            0,
        )
        both = jnp.dot(left, cut_ref[far_one], preferred_element_type=jnp.float32)
        both = both.astype(jnp.bfloat16)
        for m in range(fanout // 8):
            lanes = pl.ds(m * 128, 128)
            mine[row, :, lanes] = both[m * 128:(m + 1) * 128, :128]
            give[row, :, lanes] = both[m * 128:(m + 1) * 128, 128:]

    for g in range(GROUPS):
        loads[g].wait()
        for j in range(4):
            slice_rows(4 * g + j, j // 3)
        give_near(g).start()
        give_far(g).start()
        if g == 0:
            weight_far.start()

    def stale_rows(g, depth):
        def one(j, carry):
            row = 4 * g + j
            total = jnp.zeros((128, width), jnp.float32)
            for m in range(fanout // 8):
                left = jnp.concatenate([tiles[row, m * 8 + u] for u in range(8)], 1)
                rows = jnp.concatenate(
                    [stale[depth, old_ref[row * fanout + m * 8 + u]] for u in range(8)], 0
                )
                total = total + jnp.dot(left, rows, preferred_element_type=jnp.float32)
            old[j] = total.reshape(8, 16, width)
            return carry

        lax.fori_loop(0, 4, one, 0)

    def body(layer, carry):
        for g in range(GROUPS):
            if g == 2:
                @pl.when(layer == 0)
                def _():
                    weight_pass.wait_recv()

            for stage, back in ORDER:
                turn = g - back
                if turn >= 0:
                    @pl.when(layer < layers)
                    def _(stage=stage, turn=turn):
                        run[stage](turn, layer)
                else:
                    @pl.when(layer > 0)
                    def _(stage=stage, turn=turn):
                        run[stage](turn + GROUPS, layer - 1)

            if g == 0:
                @pl.when(layer == 0)
                def _():
                    weight_far.wait_recv()
                    weight_pass.start()
                    weight_keep.wait()
                    weight_core.wait_recv()
                    for l in range(2):
                        loads[GROUPS + l].wait()

            if g < GROUPS - 1:
                @pl.when((layer < layers) & (section == layer // 2))
                def _(g=g):
                    stale_rows(g, layer % 2)
        return carry

    run = {"a": stage_a, "d": stage_d, "e": stage_e, "h": stage_h}
    lax.fori_loop(0, layers + 1, body, 0)

    for g in range(GROUPS):
        rows = pl.ds(4 * g, 4)
        kept = fin[g][section, x_lo]
        out_ref[rows, core * 4 + x] = kept
        for n, (s, c) in enumerate(hops):
            to_out(g, n).wait_recv()
            piece = ((core + c) % 2) * 4 + (x + 4 - s) % 4
            out_ref[rows, piece] = finland[g][n]
        for n in range(len(hops)):
            to_out(g, n).wait_send()
        give_near(g).wait_send()
        give_far(g).wait_send()
    weight_core.wait_send()
    weight_far.wait_send()
    weight_pass.wait_send()


ORDER = (("a", 0), ("d", 1), ("h", 2), ("e", 1))


def run_layers(idx, picks, old, betas, tiles, stale, weights, initial, cuts, spread):
    depth, width = weights.shape[:2]
    blocks, piece = initial.shape[1:3]
    fanout, block = tiles.shape[1:3]
    dt = jnp.bfloat16
    slab = (piece, width)

    def each(shape, dtype=dt, tail=slab):
        return [pltpu.VMEM((*shape, *tail), dtype) for _ in range(GROUPS)]

    sems = pltpu.SemaphoreType.DMA
    scratch = [
        pltpu.VMEM((2, 4 * GROUPS + 97, *slab), dt),
        pltpu.VMEM((8, 8, *slab), jnp.float32),
        pltpu.VMEM((4, *weights.shape), dt),
        *[pltpu.VMEM((blocks, block, fanout * piece), dt) for _ in range(3)],
        pltpu.VMEM(tiles.shape, dt),
        pltpu.VMEM((depth, stale.shape[1] + 1, block, width), dt),
        pltpu.VMEM((4, 8, *slab), jnp.float32),
        *each((2, 4)), *each((4, 2, 4)), *each((2, 3, 2, 4)),
        *each((3, 4, 2, 2)), *each((2, 3, 4, 2, 2)),
        *each((8, 4)), *each((2, 8, 4)),
        *each((3, 8)), *each((2, 3, 8)), *each((8,), jnp.float32),
        *each((4, 2, 4), dt, (piece, 128)), *each((7, 4), dt, (piece, 128)),
        sems((9,)), sems((18,)), sems((36,)), sems((72,)), sems((3,)), sems((6,)),
        sems((9,)), sems((18,)), sems((21,)), sems((21,)), sems((6,)), sems((6,)),
        sems((3,)), sems((3,)), sems, sems((5,)),
    ]
    smem = pl.BlockSpec(memory_space=pltpu.SMEM)
    vmem = pl.BlockSpec(memory_space=pltpu.VMEM)
    hbm = pl.BlockSpec(memory_space=pltpu.MemorySpace.HBM)
    return pl.pallas_call(
        main_kernel,
        out_shape=jax.ShapeDtypeStruct((blocks, 8, piece, 128), dt),
        in_specs=[smem] * 4 + [hbm] * 2 + [vmem] * 4,
        out_specs=vmem,
        scratch_shapes=scratch,
        compiler_params=pltpu.CompilerParams(
            vmem_limit_bytes=VMEM_LIMIT, collective_id=0, has_side_effects=True
        ),
        name="run_layers",
    )(idx, picks, old, betas, tiles, stale, weights, initial, cuts, spread)


def per_device(
    initial_features, layer_weights, adjacency_tiles, tile_columns, send_blocks, stale_imports
):
    section, dom, x_hi, core, z, y, x_lo = place()
    sections = lax.axis_size("section")
    part_count = lax.axis_size("dom")
    blocks, fanout, block = adjacency_tiles.shape[:3]
    width = initial_features.shape[1]
    groups = send_blocks.shape[1]
    group_blocks = blocks // groups
    layers = layer_weights.shape[0] * sections
    piece = block // 8

    def number(hi, lo):
        return core * 4 + hi * 2 + lo

    mine = number(x_hi, x_lo)
    near, far = number(x_hi, 1 - x_lo), number(1 - x_hi, 1 - x_lo)
    swap = [(p, p + 1 - 2 * (p % 2)) for p in range(part_count)]

    def by_half(own, other):
        pair = jnp.stack([own, other])
        return jnp.where(x_lo == 0, pair, pair[::-1])

    init_blocks = initial_features.reshape(blocks, 8, piece, width)
    own_init = lax.dynamic_index_in_dim(init_blocks, mine, 1, keepdims=False)
    other_init = lax.dynamic_index_in_dim(init_blocks, near, 1, keepdims=False)
    other_init = lax.ppermute(other_init, "dom", swap)

    numbers = jnp.concatenate([send_blocks.reshape(-1), tile_columns.reshape(-1)])
    numbers = by_half(numbers, lax.ppermute(numbers, "dom", swap))
    sends = jnp.maximum(numbers[:, : groups * part_count], 0)
    columns = numbers[:, groups * part_count :].reshape(2, blocks, fanout)

    def along(step):
        moves = []
        for s in range(sections):
            for p in range(part_count):
                pz, py, lo = p // 8, (p // 2) % 4, p % 2
                q = (
                    ((pz + step) % 4) * 8 + py * 2 + lo
                    if s % 2 == 0
                    else pz * 8 + ((py + step) % 4) * 2 + lo
                )
                moves.append((s * part_count + p, s * part_count + q))
        return moves

    lines = jnp.stack(
        [sends] + [lax.ppermute(sends, ("section", "dom"), along(step)) for step in (1, 2, 3)]
    )
    a = jnp.where(core == 0, z, y)
    lines = lines[(a - jnp.arange(4, dtype=jnp.int32)) % 4]
    lines = lines.reshape(4, 2, groups, 4, 4, 2)
    to_y = lax.dynamic_index_in_dim(lines, z, 3, keepdims=False)
    to_z = lax.dynamic_index_in_dim(lines, y, 4, keepdims=False)
    picks = jnp.where(core == 0, to_y, to_z)
    picks = picks.transpose(2, 3, 4, 0, 1).reshape(-1).astype(jnp.int32)

    row_group = (jnp.arange(blocks, dtype=jnp.int32) // group_blocks)[None, :, None]
    slot = jnp.maximum(columns - blocks, 0)
    slot_group, source = slot // part_count, slot % part_count
    zs, ys, los = source // 8, (source // 2) % 4, source % 2
    where = jnp.where(core == 0, ys * 8 + zs * 2, zs * 8 + ys * 2) + los
    idx = jnp.where(
        columns < blocks,
        columns,
        jnp.where(
            slot_group <= row_group,
            blocks + slot_group * part_count + where,
            blocks + groups * part_count,
        ),
    ).reshape(-1).astype(jnp.int32)

    old_rows = (groups - 1) * group_blocks
    own_columns = tile_columns[:old_rows]
    is_old = own_columns >= blocks + part_count * (row_group[0, :old_rows] + 1)
    stale_slots = stale_imports.shape[2]
    old = jnp.where(is_old, own_columns - blocks - part_count, stale_slots).reshape(-1)

    lane = jnp.arange(2 * block, dtype=jnp.int32)
    targets = jnp.where(lane[None] < block, mine, jnp.stack([near, far])[:, None])
    wanted = ((lane % block) // piece) * block + targets * piece + lane % piece
    cuts = jnp.arange(8 * block, dtype=jnp.int32)[None, :, None] == wanted[:, None, :]

    betas = jnp.log(lambda_decay / (jnp.arange(layers, dtype=jnp.float32) + 1.0) + 1.0)
    initial = by_half(own_init, other_init)
    cols = width // sections
    source = jnp.arange(width, dtype=jnp.int32)[:, None]
    lane = jnp.arange(sections * 128, dtype=jnp.int32)[None, :]
    spread = (source == (lane // 128) * cols + lane % 128) & (lane % 128 < cols)

    done = run_layers(
        idx, picks, old, betas, adjacency_tiles, stale_imports[:, 0], layer_weights, initial,
        cuts.astype(jnp.bfloat16), spread.astype(jnp.bfloat16),
    )
    return done.reshape(blocks * block, 128)[:, :cols]


def solution(mesh):
    return jax.shard_map(
        per_device,
        mesh=mesh,
        in_specs=(
            P("dom", None),
            P("section", None, None),
            P("dom", None, None, None),
            P("dom", None),
            P("dom", None, None),
            P("section", "dom", None, None, None),
        ),
        out_specs=P("dom", "section"),
        check_vma=False,
    )
```

```python
import jax
import jax.numpy as jnp
import numpy as np
from jax import lax
from jax.experimental import pallas as pl
from jax.experimental.pallas import tpu as pltpu
from jax.sharding import PartitionSpec as P

alpha_mix = 0.1
lambda_decay = 0.5

VMEM_LIMIT = 56 * 1024 * 1024


MESH = pl.DeviceIdType.MESH
GROUPS = 3


def place():
    section, dom = lax.axis_index("section"), lax.axis_index("dom")
    x_hi, core = section // 2, section % 2
    z, y, x_lo = dom // 8, (dom // 2) % 4, dom % 2
    return section, dom, x_hi, core, z, y, x_lo


def main_kernel(
    number_ref, start_ref, tiles_ref, stale_ref, weight_ref, out_ref,
    table, part, weights, mine, give, other, tiles, stale, old,
    landed, numbers, initial, cuts, spread, *rest,
):
    rest = list(rest)

    def take(count):
        got = rest[:count]
        del rest[:count]
        return got

    xown, seltab, agbuf, out2, land2 = (take(GROUPS) for _ in range(5))
    send0, recv0, sendx, recvx, keep, fin, finland = (take(GROUPS) for _ in range(7))
    (ag_s, ag_r, sel_s, sel_r, core_s, core_r, x_s, x_r, fin_s, fin_r,
     tile_s, tile_r, w_s, w_r, w_local, load, num_s, num_r, num_local, start_s, start_r) = rest

    layers = 4 * weight_ref.shape[0]
    fanout = tiles_ref.shape[1]
    width = weight_ref.shape[1]
    section, dom, x_hi, core, z, y, x_lo = place()
    x = x_hi * 2 + x_lo
    a = (1 - core) * z + core * y
    b = (1 - core) * y + core * z

    def on_a(step, other_lo=0):
        zz, yy = (z + (1 - core) * step) % 4, (y + core * step) % 4
        return (section, zz * 8 + yy * 2 + (x_lo + other_lo) % 2)

    def on_b(step):
        zz, yy = (z + core * step) % 4, (y + (1 - core) * step) % 4
        return (section, zz * 8 + yy * 2 + x_lo)

    def on_x(step, other_core=0):
        xx = (x + step) % 4
        cc = (core + other_core) % 2
        return ((xx // 2) * 2 + cc, z * 8 + y * 2 + xx % 2)

    steps = (1, 3, 2)
    partner = on_x(0, 1)
    near = (section, z * 8 + y * 2 + 1 - x_lo)
    far = ((1 - x_hi) * 2 + core, z * 8 + y * 2 + 1 - x_lo)

    piece, near_piece = core * 4 + x, core * 4 + x_hi * 2 + 1 - x_lo
    loads = []
    for g in range(GROUPS):
        rows = pl.ds(4 * g, 4)
        loads.append(pltpu.make_async_copy(tiles_ref.at[rows], tiles.at[rows], load.at[g]))
    for l in range(2):
        loads.append(
            pltpu.make_async_copy(stale_ref.at[l], stale.at[l, pl.ds(0, 64)], load.at[GROUPS + l])
        )
    start_own = pltpu.make_async_copy(start_ref.at[:, piece], initial.at[x_lo], load.at[5])
    number_own = pltpu.make_async_copy(number_ref, numbers.at[0], num_local.at[0])
    start_own.start()
    number_own.start()
    for item in loads:
        item.start()

    barrier = pltpu.get_barrier_semaphore()
    friends = [on_a(s) for s in steps] + [on_b(s) for s in steps] + [partner]
    friends += [on_x(s, c) for s in steps for c in range(2)]
    friends += [on_a(s, 1) for s in steps]
    for friend in friends:
        pl.semaphore_signal(barrier, inc=1, device_id=friend, device_id_type=MESH)
    pl.semaphore_wait(barrier, len(friends))

    def remote(src, dst, ssem, rsem, device):
        return pltpu.make_async_remote_copy(
            src_ref=src, dst_ref=dst, send_sem=ssem, recv_sem=rsem,
            device_id=device, device_id_type=MESH,
        )

    def gather(g, par, d):
        return remote(xown[g], agbuf[g].at[par, d], ag_s.at[g * 3 + d],
                      ag_r.at[(g * 2 + par) * 3 + d], on_a(steps[d]))

    def choose(g, par, d, n):
        return remote(out2[g].at[d, n], land2[g].at[par, d, n], sel_s.at[(g * 3 + d) * 4 + n],
                      sel_r.at[((g * 2 + par) * 3 + d) * 4 + n], on_b(steps[d]))

    def to_core(g, par):
        return remote(send0[g], recv0[g].at[par], core_s.at[g], core_r.at[g * 2 + par], partner)

    def to_x(g, par, d):
        return remote(sendx[g].at[d], recvx[g].at[par, d], x_s.at[g * 3 + d],
                      x_r.at[(g * 2 + par) * 3 + d], on_x(steps[d]))

    hops = [(s, c) for s in (1, 3, 2, 0) for c in range(2) if (s, c) != (0, 0)]

    def to_out(g, n):
        s, c = hops[n]
        target = (x + s) % 4
        return remote(fin[g].at[(target // 2) * 2 + (core + c) % 2, target % 2], finland[g].at[n],
                      fin_s.at[g * 7 + n], fin_r.at[g * 7 + n], on_x(s, c))

    def give_near(g):
        rows = pl.ds(4 * g, 3)
        return remote(give.at[rows], other.at[rows], tile_s.at[g * 2], tile_r.at[g * 2], near)

    def give_far(g):
        rows = pl.ds(4 * g + 3, 1)
        return remote(give.at[rows], other.at[rows], tile_s.at[g * 2 + 1],
                      tile_r.at[g * 2 + 1], far)

    far_section = (1 - x_hi) * 2 + core
    weight_keep = pltpu.make_async_copy(weight_ref, weights.at[section], w_local)
    weight_core = remote(weight_ref, weights.at[section], w_s.at[0], w_r.at[0], partner)
    weight_far = remote(weight_ref, weights.at[section], w_s.at[1], w_r.at[1], far)
    weight_pass = remote(weights.at[far_section], weights.at[far_section], w_s.at[2], w_r.at[2],
                         partner)

    lines = [a] + [(a + 4 - step) % 4 for step in steps]
    line_stride, place_stride = 8 - 6 * core, 2 + 6 * core

    def number_to(k):
        n, flip = k // 2, k % 2
        return remote(number_ref, landed.at[k], num_s.at[k], num_r.at[k],
                      on_a(steps[n - 1] if n else 0, flip))

    def start_to(g):
        rows = pl.ds(4 * g, 4)
        return remote(start_ref.at[rows, near_piece], initial.at[x_lo, rows], start_s.at[g],
                      start_r.at[g], near)

    def chosen(g, dest, half, n, lo):
        target = a * line_stride + dest * place_stride + half
        pick = numbers[n * 2 + (lo + x_lo) % 2, 0, g * 32 + target]
        return seltab[g][n, lo, jnp.maximum(pick, 0)]

    def send_chosen(g, par, n):
        for d in (2, 0, 1):
            for half in range(2):
                for lo in range(2):
                    out2[g][d, n, half, lo] = chosen(g, (b + steps[d]) % 4, half, n, lo)
            choose(g, par, d, n).start()

    def stage_a(g, layer):
        par = layer % 2
        for d in range(3):
            gather(g, par, d).wait_recv()
            seltab[g][d + 1] = agbuf[g][par, d]
            send_chosen(g, par, d + 1)

    def slot_of(g, place_b, n):
        return 4 * GROUPS + g * 32 + place_b * place_stride + lines[n] * line_stride

    def stage_d(g, layer):
        par = layer % 2
        for half in range(2):
            table[half, pl.ds(4 * g, 4)] = xown[g][half]
            for n in range(4):
                for lo in range(2):
                    table[half, slot_of(g, b, n) + lo] = chosen(g, b, half, n, lo)
        for n in range(4):
            for d in range(3):
                choose(g, par, d, n).wait_recv()
                slots = pl.ds(slot_of(g, (b + 4 - steps[d]) % 4, n), 2)
                for half in range(2):
                    table[half, slots] = land2[g][par, d, n, half]

        @pl.when(layer == 0)
        def _():
            give_near(g).wait_recv()
            give_far(g).wait_recv()

        for rel, (cut, half) in enumerate(((mine, x_lo), (other, 1 - x_lo))):
            def row_block(j, carry, rel=rel, cut=cut, half=half):
                row = g * 4 + j

                def entry(t):
                    column = numbers[rel, 1 + row, t]
                    fresh = column < 4 * GROUPS + 32 * (g + 1)
                    return table[half, jnp.where(fresh, column, 4 * GROUPS + 96)]

                rows = jnp.concatenate([entry(t) for t in range(fanout)], 0)
                total = jnp.dot(cut[row], rows, preferred_element_type=jnp.float32)
                part[half * 4 + j] = total.reshape(8, 16, width)
                return carry

            lax.fori_loop(0, 4, row_block, 0, unroll=True)

        if g < GROUPS - 1:
            @pl.when(section == layer // 2)
            def _():
                for j in range(4):
                    part[x_lo * 4 + j] += old[j]

        for j in range(8):
            send0[g][j] = part[j, pl.ds((1 - core) * 4, 4)].astype(jnp.bfloat16)
        to_core(g, par).start()
        for d in range(3):
            gather(g, par, d).wait_send()

    def stage_e(g, layer):
        par = layer % 2
        to_core(g, par).wait_recv()

        def summed(j, piece):
            return part[j, core * 4 + piece] + recv0[g][par, j, piece].astype(jnp.float32)

        for d in (2, 0, 1):
            piece = (x + steps[d]) % 4
            for j in range(8):
                sendx[g][d, j] = summed(j, piece).astype(jnp.bfloat16)
            to_x(g, par, d).start()
        for j in range(8):
            keep[g][j] = summed(j, x)
        for d in range(3):
            for n in range(4):
                choose(g, par, d, n).wait_send()

    def stage_h(g, layer):
        par = layer % 2
        total = keep[g][...]
        for d in range(3):
            to_x(g, par, d).wait_recv()
            total = total + recvx[g][par, d].astype(jnp.float32)
        start = jnp.concatenate([initial[half, pl.ds(4 * g, 4)] for half in range(2)], 0)
        mixed = (1.0 - alpha_mix) * total + alpha_mix * start.astype(jnp.float32)
        mixed = mixed.astype(jnp.bfloat16).reshape(8 * 16, width)
        beta = jnp.float32(BETAS[0])
        for l in range(1, layers):
            beta = jnp.where(layer == l, jnp.float32(BETAS[l]), beta)
        weight = weights[layer // 2, layer % 2]
        product = jnp.dot(mixed, weight, preferred_element_type=jnp.float32)
        value = (1.0 - beta) * mixed.astype(jnp.float32) + beta * product
        value = jnp.maximum(value, 0.0).astype(jnp.bfloat16)

        @pl.when(layer < layers - 1)
        def _():
            shaped = value.reshape(2, 4, 16, width)
            xown[g][...] = shaped
            for d in (2, 0, 1):
                gather(g, 1 - par, d).start()
            seltab[g][0] = shaped
            send_chosen(g, 1 - par, 0)

        @pl.when(layer == layers - 1)
        def _():
            wide = jnp.dot(value, spread[...], preferred_element_type=jnp.float32)
            wide = wide.astype(jnp.bfloat16)
            for target in range(4):
                lanes = wide[:, target * 128:(target + 1) * 128]
                fin[g][target] = lanes.reshape(2, 4, 16, 128)
            for n in range(len(hops)):
                to_out(g, n).start()

        to_core(g, par).wait_send()
        for d in range(3):
            to_x(g, par, d).wait_send()

    for g in range(GROUPS):
        start_to(g).start()
    for k in range(1, 8):
        number_to(k).start()
    weight_keep.start()
    weight_core.start()

    for half in range(2):
        table[half, 4 * GROUPS + 96] = jnp.zeros((16, width), jnp.bfloat16)
    for l in range(2):
        stale[l, 64] = jnp.zeros((128, width), jnp.bfloat16)

    row = lax.broadcasted_iota(jnp.int32, (128, 256), 0)
    lane = lax.broadcasted_iota(jnp.int32, (128, 256), 1)
    inner = lane & 127
    for far_one in range(2):
        given = near_piece if far_one == 0 else core * 4 + (1 - x_hi) * 2 + 1 - x_lo
        wanted = jnp.where(lane < 128, piece, given) * 16 + (inner & 15)
        for u in range(8):
            hit = (inner >= u * 16) & (inner < u * 16 + 16) & (row == wanted)
            cuts[far_one, pl.ds(u * 128, 128), :] = jnp.where(hit, 1.0, 0.0).astype(jnp.bfloat16)
    cols = width // 4
    row = lax.broadcasted_iota(jnp.int32, (width, 128), 0)
    lane = lax.broadcasted_iota(jnp.int32, (width, 128), 1)
    for target in range(4):
        hit = (row == target * cols + lane) & (lane < cols)
        spread[:, pl.ds(target * 128, 128)] = jnp.where(hit, 1.0, 0.0).astype(jnp.bfloat16)

    start_own.wait()
    for g in range(GROUPS):
        start_to(g).wait_recv()
        for half in range(2):
            xown[g][half] = initial[half, pl.ds(4 * g, 4)]
        for d in (2, 0, 1):
            gather(g, 0, d).start()
        for half in range(2):
            seltab[g][0, half] = initial[half, pl.ds(4 * g, 4)]
    for k in range(1, 8):
        number_to(k).wait_recv()
    number_rest = pltpu.make_async_copy(
        landed.at[pl.ds(1, 7)], numbers.at[pl.ds(1, 7)], num_local.at[1]
    )
    number_rest.start()
    number_own.wait()
    number_rest.wait()
    for g in range(GROUPS):
        send_chosen(g, 0, 0)

    def slice_rows(row, far_one):
        left = jnp.concatenate(
            [
                jnp.concatenate([tiles[row, m * 8 + u] for u in range(8)], 1)
                for m in range(fanout // 8)
            ],
            0,
        )
        both = jnp.dot(left, cuts[far_one], preferred_element_type=jnp.float32)
        both = both.astype(jnp.bfloat16)
        for m in range(fanout // 8):
            lanes = pl.ds(m * 128, 128)
            mine[row, :, lanes] = both[m * 128:(m + 1) * 128, :128]
            give[row, :, lanes] = both[m * 128:(m + 1) * 128, 128:]

    for g in range(GROUPS):
        loads[g].wait()
        for j in range(4):
            slice_rows(4 * g + j, j // 3)
        give_near(g).start()
        give_far(g).start()
        if g == 0:
            weight_far.start()
        stage_a(g, 0)

    def stale_rows(g, depth):
        def one(j, carry):
            row = 4 * g + j
            total = jnp.zeros((128, width), jnp.float32)
            for m in range(fanout // 8):
                left = jnp.concatenate([tiles[row, m * 8 + u] for u in range(8)], 1)

                def entry(t):
                    column = numbers[0, 1 + row, t]
                    past = column - (4 * GROUPS + 32)
                    return stale[depth, jnp.where(past >= 32 * g, past, 64)]

                rows = jnp.concatenate([entry(m * 8 + u) for u in range(8)], 0)
                total = total + jnp.dot(left, rows, preferred_element_type=jnp.float32)
            old[j] = total.reshape(8, 16, width)
            return carry

        lax.fori_loop(0, 4, one, 0)

    def body(layer, carry):
        for g in range(GROUPS):
            if g == 2:
                @pl.when(layer == 0)
                def _():
                    weight_pass.wait_recv()

            for stage, back in ORDER:
                turn = g - back
                if turn >= 0:
                    @pl.when((layer < layers) & (layer > 0) if stage == "a" else layer < layers)
                    def _(stage=stage, turn=turn):
                        run[stage](turn, layer)
                else:
                    @pl.when(layer > 0)
                    def _(stage=stage, turn=turn):
                        run[stage](turn + GROUPS, layer - 1)

            if g == 0:
                @pl.when(layer == 0)
                def _():
                    weight_far.wait_recv()
                    weight_pass.start()
                    weight_keep.wait()
                    weight_core.wait_recv()
                    for l in range(2):
                        loads[GROUPS + l].wait()

            if g < GROUPS - 1:
                @pl.when((layer < layers) & (section == layer // 2))
                def _(g=g):
                    stale_rows(g, layer % 2)
        return carry

    run = {"a": stage_a, "d": stage_d, "e": stage_e, "h": stage_h}
    lax.fori_loop(0, layers + 1, body, 0)

    for g in range(GROUPS):
        rows = pl.ds(4 * g, 4)
        kept = fin[g][section, x_lo]
        out_ref[rows, core * 4 + x] = kept
        for n, (s, c) in enumerate(hops):
            to_out(g, n).wait_recv()
            piece = ((core + c) % 2) * 4 + (x + 4 - s) % 4
            out_ref[rows, piece] = finland[g][n]
        for n in range(len(hops)):
            to_out(g, n).wait_send()
        give_near(g).wait_send()
        give_far(g).wait_send()
        start_to(g).wait_send()
    for k in range(1, 8):
        number_to(k).wait_send()
    weight_core.wait_send()
    weight_far.wait_send()
    weight_pass.wait_send()


BETAS = [float(np.log(np.float32(lambda_decay / (l + 1.0)) + np.float32(1.0))) for l in range(8)]
ORDER = (("a", 0), ("d", 1), ("h", 2), ("e", 1))


def run_layers(numbers, start, tiles, stale, weights):
    depth, width = weights.shape[:2]
    blocks, pieces, piece = start.shape[:3]
    fanout, block = tiles.shape[1:3]
    dt = jnp.bfloat16
    slab = (piece, width)

    def each(shape, dtype=dt, tail=slab):
        return [pltpu.VMEM((*shape, *tail), dtype) for _ in range(GROUPS)]

    sems = pltpu.SemaphoreType.DMA
    scratch = [
        pltpu.VMEM((2, 4 * GROUPS + 97, *slab), dt),
        pltpu.VMEM((8, 8, *slab), jnp.float32),
        pltpu.VMEM((4, *weights.shape), dt),
        *[pltpu.VMEM((blocks, block, fanout * piece), dt) for _ in range(3)],
        pltpu.VMEM(tiles.shape, dt),
        pltpu.VMEM((depth, stale.shape[1] + 1, block, width), dt),
        pltpu.VMEM((4, 8, *slab), jnp.float32),
        pltpu.VMEM((8, *numbers.shape), jnp.int32),
        pltpu.SMEM((8, *numbers.shape), jnp.int32),
        pltpu.VMEM((2, blocks, *slab), dt),
        pltpu.VMEM((2, 8 * block, 2 * block), dt),
        pltpu.VMEM((width, 4 * block), dt),
        *each((2, 4)), *each((4, 2, 4)), *each((2, 3, 2, 4)),
        *each((3, 4, 2, 2)), *each((2, 3, 4, 2, 2)),
        *each((8, 4)), *each((2, 8, 4)),
        *each((3, 8)), *each((2, 3, 8)), *each((8,), jnp.float32),
        *each((4, 2, 4), dt, (piece, 128)), *each((7, 4), dt, (piece, 128)),
        sems((9,)), sems((18,)), sems((36,)), sems((72,)), sems((3,)), sems((6,)),
        sems((9,)), sems((18,)), sems((21,)), sems((21,)), sems((6,)), sems((6,)),
        sems((3,)), sems((3,)), sems, sems((6,)),
        sems((8,)), sems((8,)), sems((2,)), sems((3,)), sems((3,)),
    ]
    vmem = pl.BlockSpec(memory_space=pltpu.VMEM)
    hbm = pl.BlockSpec(memory_space=pltpu.MemorySpace.HBM)
    return pl.pallas_call(
        main_kernel,
        out_shape=jax.ShapeDtypeStruct((blocks, pieces, piece, 128), dt),
        in_specs=[hbm] * 4 + [vmem],
        out_specs=vmem,
        scratch_shapes=scratch,
        compiler_params=pltpu.CompilerParams(
            vmem_limit_bytes=VMEM_LIMIT, collective_id=0, has_side_effects=True
        ),
        name="run_layers",
    )(numbers, start, tiles, stale, weights)


def per_device(
    initial_features, layer_weights, adjacency_tiles, tile_columns, send_blocks, stale_imports
):
    blocks, fanout, block = adjacency_tiles.shape[:3]
    width = initial_features.shape[1]
    groups, part_count = send_blocks.shape[1:]
    piece = block // 8
    cols = width // 4
    sends = jnp.pad(send_blocks.reshape(1, -1), ((0, 0), (0, 128 - groups * part_count)))
    columns = jnp.pad(tile_columns, ((0, 15 - blocks), (0, 128 - fanout)))
    numbers = jnp.concatenate([sends, columns], 0)
    start = initial_features.reshape(blocks, 8, piece, width)
    done = run_layers(numbers, start, adjacency_tiles, stale_imports[:, 0], layer_weights)
    return done.reshape(blocks * block, 128)[:, :cols]


def solution(mesh):
    return jax.shard_map(
        per_device,
        mesh=mesh,
        in_specs=(
            P("dom", None),
            P("section", None, None),
            P("dom", None, None, None),
            P("dom", None),
            P("dom", None, None),
            P("section", "dom", None, None, None),
        ),
        out_specs=P("dom", "section"),
        check_vma=False,
    )
```

```python
import jax
import jax.numpy as jnp
import numpy as np
from jax import lax
from jax.experimental import pallas as pl
from jax.experimental.pallas import tpu as pltpu
from jax.sharding import PartitionSpec as P

alpha_mix = 0.1
lambda_decay = 0.5

VMEM_LIMIT = 56 * 1024 * 1024


MESH = pl.DeviceIdType.MESH
GROUPS = 3


def place():
    section, dom = lax.axis_index("section"), lax.axis_index("dom")
    x_hi, core = section // 2, section % 2
    z, y, x_lo = dom // 8, (dom // 2) % 4, dom % 2
    return section, dom, x_hi, core, z, y, x_lo


def main_kernel(
    number_ref, start_ref, tiles_ref, stale_ref, weight_ref, out_ref,
    table, part, weights, mine, give, other, tiles, stale, old,
    landed, numbers, initial, cuts, spread, *rest,
):
    rest = list(rest)

    def take(count):
        got = rest[:count]
        del rest[:count]
        return got

    xown, seltab, agbuf, out2, land2 = (take(GROUPS) for _ in range(5))
    send0, recv0, sendx, recvx, keep, fin, finland = (take(GROUPS) for _ in range(7))
    (ag_s, ag_r, sel_s, sel_r, core_s, core_r, x_s, x_r, fin_s, fin_r,
     tile_s, tile_r, w_s, w_r, w_local, load, num_s, num_r, num_local, start_s, start_r) = rest

    layers = 4 * weight_ref.shape[0]
    fanout = tiles_ref.shape[1]
    width = weight_ref.shape[1]
    section, dom, x_hi, core, z, y, x_lo = place()
    x = x_hi * 2 + x_lo
    a = (1 - core) * z + core * y
    b = (1 - core) * y + core * z

    def on_a(step, other_lo=0):
        zz, yy = (z + (1 - core) * step) % 4, (y + core * step) % 4
        return (section, zz * 8 + yy * 2 + (x_lo + other_lo) % 2)

    def on_b(step):
        zz, yy = (z + core * step) % 4, (y + (1 - core) * step) % 4
        return (section, zz * 8 + yy * 2 + x_lo)

    def on_x(step, other_core=0):
        xx = (x + step) % 4
        cc = (core + other_core) % 2
        return ((xx // 2) * 2 + cc, z * 8 + y * 2 + xx % 2)

    steps = (1, 3, 2)
    partner = on_x(0, 1)
    near = (section, z * 8 + y * 2 + 1 - x_lo)
    far = ((1 - x_hi) * 2 + core, z * 8 + y * 2 + 1 - x_lo)

    piece, near_piece = core * 4 + x, core * 4 + x_hi * 2 + 1 - x_lo
    loads = []
    for g in range(GROUPS):
        rows = pl.ds(4 * g, 4)
        loads.append(pltpu.make_async_copy(tiles_ref.at[rows], tiles.at[rows], load.at[g]))
    for l in range(2):
        loads.append(
            pltpu.make_async_copy(stale_ref.at[l], stale.at[l, pl.ds(0, 64)], load.at[GROUPS + l])
        )
    start_own = pltpu.make_async_copy(start_ref.at[:, piece], initial.at[x_lo], load.at[5])
    number_own = pltpu.make_async_copy(number_ref, numbers.at[0], num_local.at[0])
    start_own.start()
    number_own.start()
    for item in loads:
        item.start()

    barrier = pltpu.get_barrier_semaphore()
    friends = [on_a(s) for s in steps] + [on_b(s) for s in steps] + [partner]
    friends += [on_x(s, c) for s in steps for c in range(2)]
    friends += [on_a(s, 1) for s in steps]
    for friend in friends:
        pl.semaphore_signal(barrier, inc=1, device_id=friend, device_id_type=MESH)
    pl.semaphore_wait(barrier, len(friends))

    def remote(src, dst, ssem, rsem, device):
        return pltpu.make_async_remote_copy(
            src_ref=src, dst_ref=dst, send_sem=ssem, recv_sem=rsem,
            device_id=device, device_id_type=MESH,
        )

    def gather(g, par, d):
        return remote(xown[g], agbuf[g].at[par, d], ag_s.at[g * 3 + d],
                      ag_r.at[(g * 2 + par) * 3 + d], on_a(steps[d]))

    def choose(g, par, d, n):
        return remote(out2[g].at[d, n], land2[g].at[par, d, n], sel_s.at[(g * 3 + d) * 4 + n],
                      sel_r.at[((g * 2 + par) * 3 + d) * 4 + n], on_b(steps[d]))

    def to_core(g, par):
        return remote(send0[g], recv0[g].at[par], core_s.at[g], core_r.at[g * 2 + par], partner)

    def to_x(g, par, d):
        return remote(sendx[g].at[d], recvx[g].at[par, d], x_s.at[g * 3 + d],
                      x_r.at[(g * 2 + par) * 3 + d], on_x(steps[d]))

    hops = [(s, c) for s in (1, 3, 2, 0) for c in range(2) if (s, c) != (0, 0)]

    def to_out(g, n):
        s, c = hops[n]
        target = (x + s) % 4
        return remote(fin[g].at[(target // 2) * 2 + (core + c) % 2, target % 2], finland[g].at[n],
                      fin_s.at[g * 7 + n], fin_r.at[g * 7 + n], on_x(s, c))

    def give_near(g):
        rows = pl.ds(4 * g, 3)
        return remote(give.at[rows], other.at[rows], tile_s.at[g * 2], tile_r.at[g * 2], near)

    def give_far(g):
        rows = pl.ds(4 * g + 3, 1)
        return remote(give.at[rows], other.at[rows], tile_s.at[g * 2 + 1],
                      tile_r.at[g * 2 + 1], far)

    far_section = (1 - x_hi) * 2 + core
    weight_keep = pltpu.make_async_copy(weight_ref, weights.at[section], w_local)
    weight_core = remote(weight_ref, weights.at[section], w_s.at[0], w_r.at[0], partner)
    weight_far = [
        remote(weight_ref.at[d], weights.at[section, d], w_s.at[1 + d], w_r.at[1 + d], far)
        for d in range(2)
    ]
    weight_pass = [
        remote(weights.at[far_section, d], weights.at[far_section, d], w_s.at[3 + d],
               w_r.at[3 + d], partner)
        for d in range(2)
    ]

    lines = [a] + [(a + 4 - step) % 4 for step in steps]
    line_stride, place_stride = 8 - 6 * core, 2 + 6 * core

    def number_to(k):
        n, flip = k // 2, k % 2
        return remote(number_ref, landed.at[k], num_s.at[k], num_r.at[k],
                      on_a(steps[n - 1] if n else 0, flip))

    def start_to(g):
        rows = pl.ds(4 * g, 4)
        return remote(start_ref.at[rows, near_piece], initial.at[x_lo, rows], start_s.at[g],
                      start_r.at[g], near)

    def chosen(g, dest, half, n, lo):
        target = a * line_stride + dest * place_stride + half
        pick = numbers[n * 2 + (lo + x_lo) % 2, 0, g * 32 + target]
        return seltab[g][n, lo, jnp.maximum(pick, 0)]

    def send_chosen(g, par, n):
        for d in (2, 0, 1):
            for half in range(2):
                for lo in range(2):
                    out2[g][d, n, half, lo] = chosen(g, (b + steps[d]) % 4, half, n, lo)
            choose(g, par, d, n).start()

    def stage_a(g, layer):
        par = layer % 2
        for d in range(3):
            gather(g, par, d).wait_recv()
            seltab[g][d + 1] = agbuf[g][par, d]
            send_chosen(g, par, d + 1)

    def slot_of(g, place_b, n):
        return 4 * GROUPS + g * 32 + place_b * place_stride + lines[n] * line_stride

    def stage_d(g, layer):
        par = layer % 2
        for half in range(2):
            table[half, pl.ds(4 * g, 4)] = xown[g][half]
            for n in range(4):
                for lo in range(2):
                    table[half, slot_of(g, b, n) + lo] = chosen(g, b, half, n, lo)
        for n in range(4):
            for d in range(3):
                choose(g, par, d, n).wait_recv()
                slots = pl.ds(slot_of(g, (b + 4 - steps[d]) % 4, n), 2)
                for half in range(2):
                    table[half, slots] = land2[g][par, d, n, half]

        @pl.when(layer == 0)
        def _():
            give_near(g).wait_recv()
            give_far(g).wait_recv()

        for rel, (cut, half) in enumerate(((mine, x_lo), (other, 1 - x_lo))):
            def row_block(j, carry, rel=rel, cut=cut, half=half):
                row = g * 4 + j

                def entry(t):
                    column = numbers[rel, 1 + row, t]
                    fresh = column < 4 * GROUPS + 32 * (g + 1)
                    return table[half, jnp.where(fresh, column, 4 * GROUPS + 96)]

                rows = jnp.concatenate([entry(t) for t in range(fanout)], 0)
                total = jnp.dot(cut[row], rows, preferred_element_type=jnp.float32)
                part[half * 4 + j] = total.reshape(8, 16, width)
                return carry

            lax.fori_loop(0, 4, row_block, 0, unroll=True)

        if g < GROUPS - 1:
            @pl.when(section == layer // 2)
            def _():
                for j in range(4):
                    part[x_lo * 4 + j] += old[j]

        for j in range(8):
            send0[g][j] = part[j, pl.ds((1 - core) * 4, 4)].astype(jnp.bfloat16)
        to_core(g, par).start()
        for d in range(3):
            gather(g, par, d).wait_send()

    def stage_e(g, layer):
        par = layer % 2
        to_core(g, par).wait_recv()

        def summed(j, piece):
            return part[j, core * 4 + piece] + recv0[g][par, j, piece].astype(jnp.float32)

        for d in (2, 0, 1):
            piece = (x + steps[d]) % 4
            for j in range(8):
                sendx[g][d, j] = summed(j, piece).astype(jnp.bfloat16)
            to_x(g, par, d).start()
        for j in range(8):
            keep[g][j] = summed(j, x)
        for d in range(3):
            for n in range(4):
                choose(g, par, d, n).wait_send()

    def stage_h(g, layer):
        par = layer % 2
        total = keep[g][...]
        for d in range(3):
            to_x(g, par, d).wait_recv()
            total = total + recvx[g][par, d].astype(jnp.float32)
        start = jnp.concatenate([initial[half, pl.ds(4 * g, 4)] for half in range(2)], 0)
        mixed = (1.0 - alpha_mix) * total + alpha_mix * start.astype(jnp.float32)
        mixed = mixed.astype(jnp.bfloat16).reshape(8 * 16, width)
        beta = jnp.float32(BETAS[0])
        for l in range(1, layers):
            beta = jnp.where(layer == l, jnp.float32(BETAS[l]), beta)
        weight = weights[layer // 2, layer % 2]
        product = jnp.dot(mixed, weight, preferred_element_type=jnp.float32)
        value = (1.0 - beta) * mixed.astype(jnp.float32) + beta * product
        value = jnp.maximum(value, 0.0).astype(jnp.bfloat16)

        @pl.when(layer < layers - 1)
        def _():
            shaped = value.reshape(2, 4, 16, width)
            xown[g][...] = shaped
            for d in (2, 0, 1):
                gather(g, 1 - par, d).start()
            seltab[g][0] = shaped
            send_chosen(g, 1 - par, 0)

        @pl.when(layer == layers - 1)
        def _():
            wide = jnp.dot(value, spread[...], preferred_element_type=jnp.float32)
            wide = wide.astype(jnp.bfloat16)
            for target in range(4):
                lanes = wide[:, target * 128:(target + 1) * 128]
                fin[g][target] = lanes.reshape(2, 4, 16, 128)
            for n in range(len(hops)):
                to_out(g, n).start()

        to_core(g, par).wait_send()
        for d in range(3):
            to_x(g, par, d).wait_send()

    for g in range(GROUPS):
        start_to(g).start()
    for k in range(1, 8):
        number_to(k).start()
    weight_keep.start()
    weight_core.start()

    for half in range(2):
        table[half, 4 * GROUPS + 96] = jnp.zeros((16, width), jnp.bfloat16)
    for l in range(2):
        stale[l, 64] = jnp.zeros((128, width), jnp.bfloat16)

    row = lax.broadcasted_iota(jnp.int32, (128, 256), 0)
    lane = lax.broadcasted_iota(jnp.int32, (128, 256), 1)
    inner = lane & 127
    for far_one in range(2):
        given = near_piece if far_one == 0 else core * 4 + (1 - x_hi) * 2 + 1 - x_lo
        wanted = jnp.where(lane < 128, piece, given) * 16 + (inner & 15)
        for u in range(8):
            hit = (inner >= u * 16) & (inner < u * 16 + 16) & (row == wanted)
            cuts[far_one, pl.ds(u * 128, 128), :] = jnp.where(hit, 1.0, 0.0).astype(jnp.bfloat16)
    cols = width // 4
    row = lax.broadcasted_iota(jnp.int32, (width, 128), 0)
    lane = lax.broadcasted_iota(jnp.int32, (width, 128), 1)
    for target in range(4):
        hit = (row == target * cols + lane) & (lane < cols)
        spread[:, pl.ds(target * 128, 128)] = jnp.where(hit, 1.0, 0.0).astype(jnp.bfloat16)

    start_own.wait()
    for g in range(GROUPS):
        start_to(g).wait_recv()
        for half in range(2):
            xown[g][half] = initial[half, pl.ds(4 * g, 4)]
        for d in (2, 0, 1):
            gather(g, 0, d).start()
        for half in range(2):
            seltab[g][0, half] = initial[half, pl.ds(4 * g, 4)]
    for k in range(1, 8):
        number_to(k).wait_recv()
    number_rest = pltpu.make_async_copy(
        landed.at[pl.ds(1, 7)], numbers.at[pl.ds(1, 7)], num_local.at[1]
    )
    number_rest.start()
    number_own.wait()
    number_rest.wait()
    for g in range(GROUPS):
        send_chosen(g, 0, 0)

    def slice_rows(row, far_one):
        left = jnp.concatenate(
            [
                jnp.concatenate([tiles[row, m * 8 + u] for u in range(8)], 1)
                for m in range(fanout // 8)
            ],
            0,
        )
        both = jnp.dot(left, cuts[far_one], preferred_element_type=jnp.float32)
        both = both.astype(jnp.bfloat16)
        for m in range(fanout // 8):
            lanes = pl.ds(m * 128, 128)
            mine[row, :, lanes] = both[m * 128:(m + 1) * 128, :128]
            give[row, :, lanes] = both[m * 128:(m + 1) * 128, 128:]

    for g in range(GROUPS):
        loads[g].wait()
        for j in range(4):
            slice_rows(4 * g + j, j // 3)
        give_near(g).start()
        give_far(g).start()
        if g == 0:
            weight_far[0].start()
        stage_a(g, 0)

    def stale_rows(g, depth):
        def one(j, carry):
            row = 4 * g + j
            total = jnp.zeros((128, width), jnp.float32)
            for m in range(fanout // 8):
                left = jnp.concatenate([tiles[row, m * 8 + u] for u in range(8)], 1)

                def entry(t):
                    column = numbers[0, 1 + row, t]
                    past = column - (4 * GROUPS + 32)
                    return stale[depth, jnp.where(past >= 32 * g, past, 64)]

                rows = jnp.concatenate([entry(m * 8 + u) for u in range(8)], 0)
                total = total + jnp.dot(left, rows, preferred_element_type=jnp.float32)
            old[j] = total.reshape(8, 16, width)
            return carry

        lax.fori_loop(0, 4, one, 0)

    def body(layer, carry):
        for g in range(GROUPS):
            if g == 2:
                for d in range(2):
                    @pl.when(layer == d)
                    def _(d=d):
                        weight_pass[d].wait_recv()

            for stage, back in ORDER:
                turn = g - back
                if turn >= 0:
                    @pl.when((layer < layers) & (layer > 0) if stage == "a" else layer < layers)
                    def _(stage=stage, turn=turn):
                        run[stage](turn, layer)
                else:
                    @pl.when(layer > 0)
                    def _(stage=stage, turn=turn):
                        run[stage](turn + GROUPS, layer - 1)

            if g == 0:
                @pl.when(layer == 0)
                def _():
                    weight_far[0].wait_recv()
                    weight_pass[0].start()
                    weight_keep.wait()
                    weight_core.wait_recv()
                    for l in range(2):
                        loads[GROUPS + l].wait()

            if g == 0:
                @pl.when(layer == 1)
                def _():
                    weight_far[1].wait_recv()
                    weight_pass[1].start()

            if g == GROUPS - 1:
                @pl.when(layer == 0)
                def _():
                    weight_far[1].start()

            if g < GROUPS - 1:
                @pl.when((layer < layers) & (section == layer // 2))
                def _(g=g):
                    stale_rows(g, layer % 2)
        return carry

    run = {"a": stage_a, "d": stage_d, "e": stage_e, "h": stage_h}
    lax.fori_loop(0, layers + 1, body, 0)

    for g in range(GROUPS):
        rows = pl.ds(4 * g, 4)
        kept = fin[g][section, x_lo]
        out_ref[rows, core * 4 + x] = kept
        for n, (s, c) in enumerate(hops):
            to_out(g, n).wait_recv()
            piece = ((core + c) % 2) * 4 + (x + 4 - s) % 4
            out_ref[rows, piece] = finland[g][n]
        for n in range(len(hops)):
            to_out(g, n).wait_send()
        give_near(g).wait_send()
        give_far(g).wait_send()
        start_to(g).wait_send()
    for k in range(1, 8):
        number_to(k).wait_send()
    weight_core.wait_send()
    for d in range(2):
        weight_far[d].wait_send()
        weight_pass[d].wait_send()


BETAS = [float(np.log(np.float32(lambda_decay / (l + 1.0)) + np.float32(1.0))) for l in range(8)]
ORDER = (("a", 0), ("d", 1), ("h", 2), ("e", 1))


def run_layers(numbers, start, tiles, stale, weights):
    depth, width = weights.shape[:2]
    blocks, pieces, piece = start.shape[:3]
    fanout, block = tiles.shape[1:3]
    dt = jnp.bfloat16
    slab = (piece, width)

    def each(shape, dtype=dt, tail=slab):
        return [pltpu.VMEM((*shape, *tail), dtype) for _ in range(GROUPS)]

    sems = pltpu.SemaphoreType.DMA
    scratch = [
        pltpu.VMEM((2, 4 * GROUPS + 97, *slab), dt),
        pltpu.VMEM((8, 8, *slab), jnp.float32),
        pltpu.VMEM((4, *weights.shape), dt),
        *[pltpu.VMEM((blocks, block, fanout * piece), dt) for _ in range(3)],
        pltpu.VMEM(tiles.shape, dt),
        pltpu.VMEM((depth, stale.shape[1] + 1, block, width), dt),
        pltpu.VMEM((4, 8, *slab), jnp.float32),
        pltpu.VMEM((8, *numbers.shape), jnp.int32),
        pltpu.SMEM((8, *numbers.shape), jnp.int32),
        pltpu.VMEM((2, blocks, *slab), dt),
        pltpu.VMEM((2, 8 * block, 2 * block), dt),
        pltpu.VMEM((width, 4 * block), dt),
        *each((2, 4)), *each((4, 2, 4)), *each((2, 3, 2, 4)),
        *each((3, 4, 2, 2)), *each((2, 3, 4, 2, 2)),
        *each((8, 4)), *each((2, 8, 4)),
        *each((3, 8)), *each((2, 3, 8)), *each((8,), jnp.float32),
        *each((4, 2, 4), dt, (piece, 128)), *each((7, 4), dt, (piece, 128)),
        sems((9,)), sems((18,)), sems((36,)), sems((72,)), sems((3,)), sems((6,)),
        sems((9,)), sems((18,)), sems((21,)), sems((21,)), sems((6,)), sems((6,)),
        sems((5,)), sems((5,)), sems, sems((6,)),
        sems((8,)), sems((8,)), sems((2,)), sems((3,)), sems((3,)),
    ]
    vmem = pl.BlockSpec(memory_space=pltpu.VMEM)
    hbm = pl.BlockSpec(memory_space=pltpu.MemorySpace.HBM)
    return pl.pallas_call(
        main_kernel,
        out_shape=jax.ShapeDtypeStruct((blocks, pieces, piece, 128), dt),
        in_specs=[hbm] * 4 + [vmem],
        out_specs=vmem,
        scratch_shapes=scratch,
        compiler_params=pltpu.CompilerParams(
            vmem_limit_bytes=VMEM_LIMIT, collective_id=0, has_side_effects=True
        ),
        name="run_layers",
    )(numbers, start, tiles, stale, weights)


def per_device(
    initial_features, layer_weights, adjacency_tiles, tile_columns, send_blocks, stale_imports
):
    blocks, fanout, block = adjacency_tiles.shape[:3]
    width = initial_features.shape[1]
    groups, part_count = send_blocks.shape[1:]
    piece = block // 8
    cols = width // 4
    sends = jnp.pad(send_blocks.reshape(1, -1), ((0, 0), (0, 128 - groups * part_count)))
    columns = jnp.pad(tile_columns, ((0, 15 - blocks), (0, 128 - fanout)))
    numbers = jnp.concatenate([sends, columns], 0)
    start = initial_features.reshape(blocks, 8, piece, width)
    done = run_layers(numbers, start, adjacency_tiles, stale_imports[:, 0], layer_weights)
    return done.reshape(blocks * block, 128)[:, :cols]


def solution(mesh):
    return jax.shard_map(
        per_device,
        mesh=mesh,
        in_specs=(
            P("dom", None),
            P("section", None, None),
            P("dom", None, None, None),
            P("dom", None),
            P("dom", None, None),
            P("section", "dom", None, None, None),
        ),
        out_specs=P("dom", "section"),
        check_vma=False,
    )
```

```python
import jax
import jax.numpy as jnp
import numpy as np
from jax import lax
from jax.experimental import pallas as pl
from jax.experimental.pallas import tpu as pltpu
from jax.sharding import PartitionSpec as P

alpha_mix = 0.1
lambda_decay = 0.5

VMEM_LIMIT = 56 * 1024 * 1024


MESH = pl.DeviceIdType.MESH
GROUPS = 3


def place():
    section, dom = lax.axis_index("section"), lax.axis_index("dom")
    x_hi, core = section // 2, section % 2
    z, y, x_lo = dom // 8, (dom // 2) % 4, dom % 2
    return section, dom, x_hi, core, z, y, x_lo


def main_kernel(
    number_ref, start_ref, tiles_ref, stale_ref, weight_ref, out_ref,
    table, part, weights, mine, give, other, tiles, stale, old,
    landed, numbers, initial, cuts, spread, *rest,
):
    rest = list(rest)

    def take(count):
        got = rest[:count]
        del rest[:count]
        return got

    xown, seltab, agbuf, out2, land2 = (take(GROUPS) for _ in range(5))
    send0, recv0, sendx, recvx, keep, fin, finland = (take(GROUPS) for _ in range(7))
    (ag_s, ag_r, sel_s, sel_r, core_s, core_r, x_s, x_r, fin_s, fin_r,
     tile_s, tile_r, w_s, w_r, w_local, load, num_s, num_r, num_local, start_s, start_r) = rest

    layers = 4 * weight_ref.shape[0]
    fanout = tiles_ref.shape[1]
    width = weight_ref.shape[1]
    section, dom, x_hi, core, z, y, x_lo = place()
    x = x_hi * 2 + x_lo
    a = (1 - core) * z + core * y
    b = (1 - core) * y + core * z

    def on_a(step, other_lo=0):
        zz, yy = (z + (1 - core) * step) % 4, (y + core * step) % 4
        return (section, zz * 8 + yy * 2 + (x_lo + other_lo) % 2)

    def on_b(step):
        zz, yy = (z + core * step) % 4, (y + (1 - core) * step) % 4
        return (section, zz * 8 + yy * 2 + x_lo)

    def on_x(step, other_core=0):
        xx = (x + step) % 4
        cc = (core + other_core) % 2
        return ((xx // 2) * 2 + cc, z * 8 + y * 2 + xx % 2)

    steps = (1, 3, 2)
    partner = on_x(0, 1)
    near = (section, z * 8 + y * 2 + 1 - x_lo)
    far = ((1 - x_hi) * 2 + core, z * 8 + y * 2 + 1 - x_lo)

    piece, near_piece = core * 4 + x, core * 4 + x_hi * 2 + 1 - x_lo
    loads = []
    for g in range(GROUPS):
        rows = pl.ds(4 * g, 4)
        loads.append(pltpu.make_async_copy(tiles_ref.at[rows], tiles.at[rows], load.at[g]))
    for l in range(2):
        loads.append(
            pltpu.make_async_copy(stale_ref.at[l], stale.at[l, pl.ds(0, 64)], load.at[GROUPS + l])
        )
    start_own = pltpu.make_async_copy(start_ref.at[:, piece], initial.at[x_lo], load.at[5])
    number_own = pltpu.make_async_copy(number_ref, numbers.at[0], num_local.at[0])
    start_own.start()
    number_own.start()
    for item in loads:
        item.start()

    barrier = pltpu.get_barrier_semaphore()
    friends = [on_a(s) for s in steps] + [on_b(s) for s in steps] + [partner]
    friends += [on_x(s, c) for s in steps for c in range(2)]
    friends += [on_a(s, 1) for s in steps]
    for friend in friends:
        pl.semaphore_signal(barrier, inc=1, device_id=friend, device_id_type=MESH)
    pl.semaphore_wait(barrier, len(friends))

    def remote(src, dst, ssem, rsem, device):
        return pltpu.make_async_remote_copy(
            src_ref=src, dst_ref=dst, send_sem=ssem, recv_sem=rsem,
            device_id=device, device_id_type=MESH,
        )

    def gather(g, par, d):
        return remote(xown[g], agbuf[g].at[par, d], ag_s.at[g * 3 + d],
                      ag_r.at[(g * 2 + par) * 3 + d], on_a(steps[d]))

    def choose(g, par, d, n):
        return remote(out2[g].at[d, n], land2[g].at[par, d, n], sel_s.at[(g * 3 + d) * 4 + n],
                      sel_r.at[((g * 2 + par) * 3 + d) * 4 + n], on_b(steps[d]))

    def to_core(g, par):
        return remote(send0[g], recv0[g].at[par], core_s.at[g], core_r.at[g * 2 + par], partner)

    def to_x(g, par, d):
        return remote(sendx[g].at[d], recvx[g].at[par, d], x_s.at[g * 3 + d],
                      x_r.at[(g * 2 + par) * 3 + d], on_x(steps[d]))

    hops = [(s, c) for s in (1, 3, 2, 0) for c in range(2) if (s, c) != (0, 0)]

    def to_out(g, n):
        s, c = hops[n]
        target = (x + s) % 4
        return remote(fin[g].at[(target // 2) * 2 + (core + c) % 2, target % 2], finland[g].at[n],
                      fin_s.at[g * 7 + n], fin_r.at[g * 7 + n], on_x(s, c))

    def give_near(g):
        rows = pl.ds(4 * g, 3)
        return remote(give.at[rows], other.at[rows], tile_s.at[g * 2], tile_r.at[g * 2], near)

    def give_far(g):
        rows = pl.ds(4 * g + 3, 1)
        return remote(give.at[rows], other.at[rows], tile_s.at[g * 2 + 1],
                      tile_r.at[g * 2 + 1], far)

    far_section = (1 - x_hi) * 2 + core
    weight_keep = pltpu.make_async_copy(weight_ref, weights.at[section], w_local)
    weight_core = remote(weight_ref, weights.at[section], w_s.at[0], w_r.at[0], partner)
    weight_far = [
        remote(weight_ref.at[d], weights.at[section, d], w_s.at[1 + d], w_r.at[1 + d], far)
        for d in range(2)
    ]
    weight_pass = [
        remote(weights.at[far_section, d], weights.at[far_section, d], w_s.at[3 + d],
               w_r.at[3 + d], partner)
        for d in range(2)
    ]

    lines = [a] + [(a + 4 - step) % 4 for step in steps]
    line_stride, place_stride = 8 - 6 * core, 2 + 6 * core

    def number_to(k):
        n, flip = k // 2, k % 2
        return remote(number_ref, landed.at[k], num_s.at[k], num_r.at[k],
                      on_a(steps[n - 1] if n else 0, flip))

    def start_to(g):
        rows = pl.ds(4 * g, 4)
        return remote(start_ref.at[rows, near_piece], initial.at[x_lo, rows], start_s.at[g],
                      start_r.at[g], near)

    def chosen(g, dest, half, n, lo):
        target = a * line_stride + dest * place_stride + half
        pick = numbers[n * 2 + (lo + x_lo) % 2, 0, g * 32 + target]
        return seltab[g][n, lo, jnp.maximum(pick, 0)]

    def send_chosen(g, par, n):
        for d in (2, 0, 1):
            for half in range(2):
                for lo in range(2):
                    out2[g][d, n, half, lo] = chosen(g, (b + steps[d]) % 4, half, n, lo)
            choose(g, par, d, n).start()

    def stage_a(g, layer):
        par = layer % 2
        send_chosen(g, par, 0)
        for d in range(3):
            gather(g, par, d).wait_recv()
            seltab[g][d + 1] = agbuf[g][par, d]
            send_chosen(g, par, d + 1)

    def slot_of(g, place_b, n):
        return 4 * GROUPS + g * 32 + place_b * place_stride + lines[n] * line_stride

    def stage_d(g, layer):
        par = layer % 2
        for half in range(2):
            table[half, pl.ds(4 * g, 4)] = xown[g][half]
            for n in range(4):
                for lo in range(2):
                    table[half, slot_of(g, b, n) + lo] = chosen(g, b, half, n, lo)
        for n in range(4):
            for d in range(3):
                choose(g, par, d, n).wait_recv()
                slots = pl.ds(slot_of(g, (b + 4 - steps[d]) % 4, n), 2)
                for half in range(2):
                    table[half, slots] = land2[g][par, d, n, half]

        @pl.when(layer == 0)
        def _():
            give_near(g).wait_recv()
            give_far(g).wait_recv()

        for rel, (cut, half) in enumerate(((mine, x_lo), (other, 1 - x_lo))):
            def row_block(j, carry, rel=rel, cut=cut, half=half):
                row = g * 4 + j

                def entry(t):
                    column = numbers[rel, 1 + row, t]
                    fresh = column < 4 * GROUPS + 32 * (g + 1)
                    return table[half, jnp.where(fresh, column, 4 * GROUPS + 96)]

                rows = jnp.concatenate([entry(t) for t in range(fanout)], 0)
                total = jnp.dot(cut[row], rows, preferred_element_type=jnp.float32)
                part[half * 4 + j] = total.reshape(8, 16, width)
                return carry

            lax.fori_loop(0, 4, row_block, 0, unroll=True)

        if g < GROUPS - 1:
            @pl.when(section == layer // 2)
            def _():
                for j in range(4):
                    part[x_lo * 4 + j] += old[j]

        for j in range(8):
            send0[g][j] = part[j, pl.ds((1 - core) * 4, 4)].astype(jnp.bfloat16)
        to_core(g, par).start()
        for d in range(3):
            gather(g, par, d).wait_send()

    def stage_e(g, layer):
        par = layer % 2
        to_core(g, par).wait_recv()

        def summed(j, piece):
            return part[j, core * 4 + piece] + recv0[g][par, j, piece].astype(jnp.float32)

        for d in (2, 0, 1):
            piece = (x + steps[d]) % 4
            for j in range(8):
                sendx[g][d, j] = summed(j, piece).astype(jnp.bfloat16)
            to_x(g, par, d).start()
        for j in range(8):
            keep[g][j] = summed(j, x)
        for d in range(3):
            for n in range(4):
                choose(g, par, d, n).wait_send()

    def stage_h(g, layer):
        par = layer % 2
        total = keep[g][...]
        for d in range(3):
            to_x(g, par, d).wait_recv()
            total = total + recvx[g][par, d].astype(jnp.float32)
        start = jnp.concatenate([initial[half, pl.ds(4 * g, 4)] for half in range(2)], 0)
        mixed = (1.0 - alpha_mix) * total + alpha_mix * start.astype(jnp.float32)
        mixed = mixed.astype(jnp.bfloat16).reshape(8 * 16, width)
        beta = jnp.float32(BETAS[0])
        for l in range(1, layers):
            beta = jnp.where(layer == l, jnp.float32(BETAS[l]), beta)
        weight = weights[layer // 2, layer % 2]
        product = jnp.dot(mixed, weight, preferred_element_type=jnp.float32)
        value = (1.0 - beta) * mixed.astype(jnp.float32) + beta * product
        value = jnp.maximum(value, 0.0).astype(jnp.bfloat16)

        @pl.when(layer < layers - 1)
        def _():
            shaped = value.reshape(2, 4, 16, width)
            xown[g][...] = shaped
            for d in (2, 0, 1):
                gather(g, 1 - par, d).start()
            seltab[g][0] = shaped

        @pl.when(layer == layers - 1)
        def _():
            wide = jnp.dot(value, spread[...], preferred_element_type=jnp.float32)
            wide = wide.astype(jnp.bfloat16)
            for target in range(4):
                lanes = wide[:, target * 128:(target + 1) * 128]
                fin[g][target] = lanes.reshape(2, 4, 16, 128)
            for n in range(len(hops)):
                to_out(g, n).start()

        to_core(g, par).wait_send()
        for d in range(3):
            to_x(g, par, d).wait_send()

    for g in range(GROUPS):
        start_to(g).start()
    for k in range(1, 8):
        number_to(k).start()
    weight_keep.start()
    weight_core.start()

    for half in range(2):
        table[half, 4 * GROUPS + 96] = jnp.zeros((16, width), jnp.bfloat16)
    for l in range(2):
        stale[l, 64] = jnp.zeros((128, width), jnp.bfloat16)

    row = lax.broadcasted_iota(jnp.int32, (128, 256), 0)
    lane = lax.broadcasted_iota(jnp.int32, (128, 256), 1)
    inner = lane & 127
    for far_one in range(2):
        given = near_piece if far_one == 0 else core * 4 + (1 - x_hi) * 2 + 1 - x_lo
        wanted = jnp.where(lane < 128, piece, given) * 16 + (inner & 15)
        for u in range(8):
            hit = (inner >= u * 16) & (inner < u * 16 + 16) & (row == wanted)
            cuts[far_one, pl.ds(u * 128, 128), :] = jnp.where(hit, 1.0, 0.0).astype(jnp.bfloat16)
    cols = width // 4
    row = lax.broadcasted_iota(jnp.int32, (width, 128), 0)
    lane = lax.broadcasted_iota(jnp.int32, (width, 128), 1)
    for target in range(4):
        hit = (row == target * cols + lane) & (lane < cols)
        spread[:, pl.ds(target * 128, 128)] = jnp.where(hit, 1.0, 0.0).astype(jnp.bfloat16)

    start_own.wait()
    for g in range(GROUPS):
        start_to(g).wait_recv()
        for half in range(2):
            xown[g][half] = initial[half, pl.ds(4 * g, 4)]
        for d in (2, 0, 1):
            gather(g, 0, d).start()
        for half in range(2):
            seltab[g][0, half] = initial[half, pl.ds(4 * g, 4)]
    for k in range(1, 8):
        number_to(k).wait_recv()
    number_rest = pltpu.make_async_copy(
        landed.at[pl.ds(1, 7)], numbers.at[pl.ds(1, 7)], num_local.at[1]
    )
    number_rest.start()
    number_own.wait()
    number_rest.wait()
    def slice_rows(row, far_one):
        left = jnp.concatenate(
            [
                jnp.concatenate([tiles[row, m * 8 + u] for u in range(8)], 1)
                for m in range(fanout // 8)
            ],
            0,
        )
        both = jnp.dot(left, cuts[far_one], preferred_element_type=jnp.float32)
        both = both.astype(jnp.bfloat16)
        for m in range(fanout // 8):
            lanes = pl.ds(m * 128, 128)
            mine[row, :, lanes] = both[m * 128:(m + 1) * 128, :128]
            give[row, :, lanes] = both[m * 128:(m + 1) * 128, 128:]

    for g in range(GROUPS):
        loads[g].wait()
        for j in range(4):
            slice_rows(4 * g + j, j // 3)
        give_near(g).start()
        give_far(g).start()
        if g == 0:
            weight_far[0].start()
        stage_a(g, 0)

    def stale_rows(g, depth):
        def one(j, carry):
            row = 4 * g + j
            total = jnp.zeros((128, width), jnp.float32)
            for m in range(fanout // 8):
                left = jnp.concatenate([tiles[row, m * 8 + u] for u in range(8)], 1)

                def entry(t):
                    column = numbers[0, 1 + row, t]
                    past = column - (4 * GROUPS + 32)
                    return stale[depth, jnp.where(past >= 32 * g, past, 64)]

                rows = jnp.concatenate([entry(m * 8 + u) for u in range(8)], 0)
                total = total + jnp.dot(left, rows, preferred_element_type=jnp.float32)
            old[j] = total.reshape(8, 16, width)
            return carry

        lax.fori_loop(0, 4, one, 0)

    def body(layer, carry):
        for g in range(GROUPS):
            if g == 2:
                for d in range(2):
                    @pl.when(layer == d)
                    def _(d=d):
                        weight_pass[d].wait_recv()

            for stage, back in ORDER:
                turn = g - back
                if turn >= 0:
                    @pl.when((layer < layers) & (layer > 0) if stage == "a" else layer < layers)
                    def _(stage=stage, turn=turn):
                        run[stage](turn, layer)
                else:
                    @pl.when(layer > 0)
                    def _(stage=stage, turn=turn):
                        run[stage](turn + GROUPS, layer - 1)

            if g == 0:
                @pl.when(layer == 0)
                def _():
                    weight_far[0].wait_recv()
                    weight_pass[0].start()
                    weight_keep.wait()
                    weight_core.wait_recv()
                    for l in range(2):
                        loads[GROUPS + l].wait()

            if g == 0:
                @pl.when(layer == 1)
                def _():
                    weight_far[1].wait_recv()
                    weight_pass[1].start()

            if g == GROUPS - 1:
                @pl.when(layer == 0)
                def _():
                    weight_far[1].start()

            if g < GROUPS - 1:
                @pl.when((layer < layers) & (section == layer // 2))
                def _(g=g):
                    stale_rows(g, layer % 2)
        return carry

    run = {"a": stage_a, "d": stage_d, "e": stage_e, "h": stage_h}
    lax.fori_loop(0, layers + 1, body, 0)

    for g in range(GROUPS):
        rows = pl.ds(4 * g, 4)
        kept = fin[g][section, x_lo]
        out_ref[rows, core * 4 + x] = kept
        for n, (s, c) in enumerate(hops):
            to_out(g, n).wait_recv()
            piece = ((core + c) % 2) * 4 + (x + 4 - s) % 4
            out_ref[rows, piece] = finland[g][n]
        for n in range(len(hops)):
            to_out(g, n).wait_send()
        give_near(g).wait_send()
        give_far(g).wait_send()
        start_to(g).wait_send()
    for k in range(1, 8):
        number_to(k).wait_send()
    weight_core.wait_send()
    for d in range(2):
        weight_far[d].wait_send()
        weight_pass[d].wait_send()


BETAS = [float(np.log(np.float32(lambda_decay / (l + 1.0)) + np.float32(1.0))) for l in range(8)]
ORDER = (("a", 0), ("d", 1), ("h", 2), ("e", 1))


def run_layers(numbers, start, tiles, stale, weights):
    depth, width = weights.shape[:2]
    blocks, pieces, piece = start.shape[:3]
    fanout, block = tiles.shape[1:3]
    dt = jnp.bfloat16
    slab = (piece, width)

    def each(shape, dtype=dt, tail=slab):
        return [pltpu.VMEM((*shape, *tail), dtype) for _ in range(GROUPS)]

    sems = pltpu.SemaphoreType.DMA
    scratch = [
        pltpu.VMEM((2, 4 * GROUPS + 97, *slab), dt),
        pltpu.VMEM((8, 8, *slab), jnp.float32),
        pltpu.VMEM((4, *weights.shape), dt),
        *[pltpu.VMEM((blocks, block, fanout * piece), dt) for _ in range(3)],
        pltpu.VMEM(tiles.shape, dt),
        pltpu.VMEM((depth, stale.shape[1] + 1, block, width), dt),
        pltpu.VMEM((4, 8, *slab), jnp.float32),
        pltpu.VMEM((8, *numbers.shape), jnp.int32),
        pltpu.SMEM((8, *numbers.shape), jnp.int32),
        pltpu.VMEM((2, blocks, *slab), dt),
        pltpu.VMEM((2, 8 * block, 2 * block), dt),
        pltpu.VMEM((width, 4 * block), dt),
        *each((2, 4)), *each((4, 2, 4)), *each((2, 3, 2, 4)),
        *each((3, 4, 2, 2)), *each((2, 3, 4, 2, 2)),
        *each((8, 4)), *each((2, 8, 4)),
        *each((3, 8)), *each((2, 3, 8)), *each((8,), jnp.float32),
        *each((4, 2, 4), dt, (piece, 128)), *each((7, 4), dt, (piece, 128)),
        sems((9,)), sems((18,)), sems((36,)), sems((72,)), sems((3,)), sems((6,)),
        sems((9,)), sems((18,)), sems((21,)), sems((21,)), sems((6,)), sems((6,)),
        sems((5,)), sems((5,)), sems, sems((6,)),
        sems((8,)), sems((8,)), sems((2,)), sems((3,)), sems((3,)),
    ]
    vmem = pl.BlockSpec(memory_space=pltpu.VMEM)
    hbm = pl.BlockSpec(memory_space=pltpu.MemorySpace.HBM)
    return pl.pallas_call(
        main_kernel,
        out_shape=jax.ShapeDtypeStruct((blocks, pieces, piece, 128), dt),
        in_specs=[hbm] * 4 + [vmem],
        out_specs=vmem,
        scratch_shapes=scratch,
        compiler_params=pltpu.CompilerParams(
            vmem_limit_bytes=VMEM_LIMIT, collective_id=0, has_side_effects=True
        ),
        name="run_layers",
    )(numbers, start, tiles, stale, weights)


def per_device(
    initial_features, layer_weights, adjacency_tiles, tile_columns, send_blocks, stale_imports
):
    blocks, fanout, block = adjacency_tiles.shape[:3]
    width = initial_features.shape[1]
    groups, part_count = send_blocks.shape[1:]
    piece = block // 8
    cols = width // 4
    sends = jnp.pad(send_blocks.reshape(1, -1), ((0, 0), (0, 128 - groups * part_count)))
    columns = jnp.pad(tile_columns, ((0, 15 - blocks), (0, 128 - fanout)))
    numbers = jnp.concatenate([sends, columns], 0)
    start = initial_features.reshape(blocks, 8, piece, width)
    done = run_layers(numbers, start, adjacency_tiles, stale_imports[:, 0], layer_weights)
    return done.reshape(blocks * block, 128)[:, :cols]


def solution(mesh):
    return jax.shard_map(
        per_device,
        mesh=mesh,
        in_specs=(
            P("dom", None),
            P("section", None, None),
            P("dom", None, None, None),
            P("dom", None),
            P("dom", None, None),
            P("section", "dom", None, None, None),
        ),
        out_specs=P("dom", "section"),
        check_vma=False,
    )
```
